128 devices in a mesh: gx: 16 (over y_hi, z, core), gy: 8 (over y_lo, x).
Axes of the slice: x: 4, y: 4 (y_hi: 2, y_lo: 2; y = y_hi * 2 + y_lo), z: 4, core: 2. Of those that a mesh axis runs over, the one named last changes fastest.
Arguments:
- prev_wave: float32 [32, 512, 4096], P(None, 'gy', 'gx'), may hold values from -6 to 6
- source: float32 [32, 512, 4096], P(None, 'gy', 'gx'), may hold values from -6 to 6
- start_state: float32 [512, 4096], P('gy', 'gx'), may hold values from -6 to 6
- storage: float32 [512, 4096], P('gy', 'gx'), may hold values from 0.5 to 4
- leakage: float32 [512, 4096], P('gy', 'gx'), may hold values from 0.1 to 1
- cond_east: float32 [512, 4096], P('gy', 'gx'), may hold values from 0.5 to 2
- cond_south: float32 [512, 4096], P('gy', 'gx'), may hold values from 0.5 to 2
- owner_weight: int32 [512, 4096], P('gy', 'gx'), may hold values from 1 to 3
- aggregate: int32 [512, 4096], P('gy', 'gx'), may hold values from 0 to 8191, as said below
- coarse_inverse: float32 [8192, 8192], P(('gx', 'gy')), as said below
Outputs:
- relaxed: float32 [32, 512, 4096], P(None, 'gy', 'gx')
The draws below stay inside these ranges and needn't reach their ends.
Inputs may be any that keep to these rules, and one draw needn't show every extreme that they name: coarse_inverse is exactly symmetric, with diagonal entries from 1 / 256 to 4 / 256. `aggregate`: the nodes of tile (a, b) carry exactly the aggregates (b * 8 + a) * 64 to (b * 8 + a + 1) * 64 - 1, each of them inside that tile.
All inputs are finite; a program needn't handle non-finite values.
Results may differ from the reference program's by a relative error of at most 0.0003.
Values sent between devices are 32-bit elements; how exact they have to be, the bound alone decides.
No kernel may reach another device: no remote copies, remote signals or barrier semaphores. Data moves between devices by JAX's collectives and lax.ppermute only.
A program may use at most 128 MiB of HBM per device.

```python
import math
import jax
import jax.numpy as jnp
from jax import lax

RD = 64
CD = 256
NT = 32
DEG = 8
OV = 2
AGG_ROWS = 8
AGG_COLS = 8
AGG_DEV = 64
NR = 512
NC = 4096
GROUP_COUNT = 8192
NODES_PER_GROUP = 256
N_GX = 16
N_GY = 8


def draw_coarse_inverse(key, part):
    first_key = jax.random.fold_in(key, 11)
    second_key = jax.random.fold_in(key, 12)
    unscaled_values = jax.random.normal(first_key, (GROUP_COUNT, GROUP_COUNT), jnp.float32)
    diagonal_entries = jnp.exp(jax.random.uniform(second_key, (GROUP_COUNT,), jnp.float32, 0.0, 1.3862943))
    offdiagonal_entries = (unscaled_values + unscaled_values.T) * (0.7 / (NODES_PER_GROUP * jnp.sqrt(jnp.float32(GROUP_COUNT))))
    identity_pattern_mask = jnp.eye(GROUP_COUNT, dtype=jnp.float32)
    return offdiagonal_entries * (1.0 - identity_pattern_mask) + identity_pattern_mask * (diagonal_entries / NODES_PER_GROUP)[:, None]


def draw_aggregate(key, part):
    row_key = jax.random.fold_in(key, 21)
    col_key = jax.random.fold_in(key, 22)
    rows = lax.broadcasted_iota(jnp.int32, (NR, NC), 0)
    cols = lax.broadcasted_iota(jnp.int32, (NR, NC), 1)
    tile_row = rows // RD
    tile_col = cols // CD
    inner_row = rows % RD
    inner_col = cols % CD
    jitter_row = jax.random.randint(row_key, (NR, NC), -1, 2, dtype=jnp.int32)
    jitter_col = jax.random.randint(col_key, (NR, NC), -2, 3, dtype=jnp.int32)
    moved_row = jnp.clip(inner_row + jitter_row, 0, RD - 1)
    moved_col = jnp.clip(inner_col + jitter_col, 0, CD - 1)
    patch = moved_row * AGG_ROWS // RD * AGG_COLS + moved_col * AGG_COLS // CD
    owner = tile_col * (NR // RD) + tile_row
    return (owner * AGG_DEV + patch).astype(jnp.int32)


def touch_ends(drawn, rng, low, largest):
    longest = drawn.shape.index(max(drawn.shape))
    spots = []
    for shift in (0, 1):
        where = [jax.random.randint(jax.random.fold_in(rng, axis), (), 0, length) for axis, length in enumerate(drawn.shape)]
        where[longest] = (where[longest] + shift) % drawn.shape[longest]
        spots.append(tuple(where))
    return drawn.at[spots[0]].set(low).at[spots[1]].set(largest)


def steps_of(key, extent, pieces, smallest, top_value):
    loudness = 1.0
    for dim, parts in pieces:
        heights = jax.random.uniform(jax.random.fold_in(jax.random.fold_in(key, 6), dim), (parts,), jnp.float32, smallest / len(pieces), top_value / len(pieces))
        loudness = loudness * jnp.repeat(jnp.exp(heights), extent[dim] // parts).reshape((-1,) + (1,) * (len(extent) - 1 - dim))
    return loudness


def scatter_about(own_key, shape, deviation, bound, pieces=(), held_as=jnp.bfloat16):
    drawn = deviation * jax.random.normal(own_key, shape, jnp.float32)
    if pieces:
        drawn = drawn * steps_of(own_key, shape, pieces, -0.22, 0.18)
    return jnp.clip(drawn, -bound, bound).astype(held_as)


def setup_inputs(seed: int = 0) -> dict:
    key_of = jax.random.split(jax.random.key(seed), 11)
    prev_wave = scatter_about(key_of[0], (NT, NR, NC), 1.0, 6.0, ((1, 8), (2, 16)), jnp.float32)
    source = scatter_about(key_of[1], (NT, NR, NC), 1.0, 6.0, ((1, 8), (2, 16)), jnp.float32)
    start_state = scatter_about(key_of[2], (NR, NC), 1.0, 6.0, ((0, 8), (1, 16)), jnp.float32)
    storage = jnp.clip(jnp.exp(math.log(4.0) - 2.0794415 * jax.random.uniform(key_of[3], (NR, NC), jnp.float32) ** steps_of(key_of[3], (NR, NC), ((0, 8), (1, 16)), -0.2, 0.2)), 0.5, 4.0)
    leakage = jnp.clip(jnp.exp(math.log(1.0) - 2.3025851 * jax.random.uniform(key_of[4], (NR, NC), jnp.float32) ** steps_of(key_of[4], (NR, NC), ((0, 8), (1, 16)), -0.2, 0.2)), 0.1, 1.0)
    cond_east = jnp.clip(jnp.exp(math.log(2.0) - 1.3862944 * jax.random.uniform(key_of[5], (NR, NC), jnp.float32) ** steps_of(key_of[5], (NR, NC), ((0, 8), (1, 16)), -0.2, 0.2)), 0.5, 2.0)
    cond_south = jnp.clip(jnp.exp(math.log(2.0) - 1.3862944 * jax.random.uniform(key_of[6], (NR, NC), jnp.float32) ** steps_of(key_of[6], (NR, NC), ((0, 8), (1, 16)), -0.2, 0.2)), 0.5, 2.0)
    owner_weight = touch_ends(jax.random.randint(key_of[7], (NR, NC), 1, 4), jax.random.fold_in(key_of[7], 1), 1, 3).astype(jnp.int32)
    aggregate = draw_aggregate(jax.random.fold_in(key_of[10], 71), 0)
    coarse_inverse = draw_coarse_inverse(jax.random.fold_in(key_of[10], 71), 0)
    return dict(prev_wave=prev_wave, source=source, start_state=start_state, storage=storage, leakage=leakage, cond_east=cond_east, cond_south=cond_south, owner_weight=owner_weight, aggregate=aggregate, coarse_inverse=coarse_inverse)


cheb_theta = 1.0
cheb_delta = 0.95


def apply_operator(full, diagonal_mid, east_mid, east_west, south_mid, south_north):
    centre = full[1:-1, 1:-1]
    return (diagonal_mid * centre - east_mid * full[1:-1, 2:] - east_west * full[1:-1, :-2]
            - south_mid * full[2:, 1:-1] - south_north * full[:-2, 1:-1])


def local_sweep(stack, steps_count):
    prev_full = stack[:steps_count]
    source_mid = stack[steps_count:2 * steps_count, 1:-1, 1:-1]
    start_mid = stack[2 * steps_count, 1:-1, 1:-1]
    storage_full = stack[2 * steps_count + 1]
    leakage_full = stack[2 * steps_count + 2]
    east_full = stack[2 * steps_count + 3]
    south_full = stack[2 * steps_count + 4]
    present_full = stack[2 * steps_count + 5]
    east_mid = east_full[1:-1, 1:-1]
    east_west = east_full[1:-1, :-2]
    south_mid = south_full[1:-1, 1:-1]
    south_north = south_full[:-2, 1:-1]
    storage_mid = storage_full[1:-1, 1:-1]
    diagonal_mid = (storage_mid + leakage_full[1:-1, 1:-1] + east_mid + east_west + south_mid
                    + south_north + (1.0 - present_full[1:-1, 1:-1]))
    inner_mask = jnp.pad(jnp.ones_like(storage_mid), 1) > 0.5
    sigma = cheb_theta / cheb_delta

    def advance(carried, inputs):
        cycle_full, source_now = inputs
        rhs = source_now + storage_mid * carried

        def residual_of(interior):
            full = jnp.where(inner_mask, jnp.pad(interior, 1), cycle_full)
            return rhs - apply_operator(full, diagonal_mid, east_mid, east_west, south_mid, south_north)

        iterate = cycle_full[1:-1, 1:-1]
        update = residual_of(iterate) / diagonal_mid / cheb_theta
        iterate = iterate + update
        rho_prev = 1.0 / sigma
        for degree in range(1, DEG):
            rho_now = 1.0 / (2.0 * sigma - rho_prev)
            update = rho_now * rho_prev * update + (2.0 * rho_now / cheb_delta) * (residual_of(iterate) / diagonal_mid)
            iterate = iterate + update
            rho_prev = rho_now
        return iterate, iterate

    final_state, waves = lax.scan(advance, start_mid, (prev_full, source_mid), unroll=8)
    return waves


def tile_shift(values, down, right):
    padded = jnp.pad(values, ((1, 1), (1, 1)) + ((0, 0),) * (values.ndim - 2))
    return padded[1 - down:1 - down + values.shape[0], 1 - right:1 - right + values.shape[1]]


def gather_rims(folded):
    extended_rows = RD + 2 * OV
    ext_cols = CD + 2 * OV
    incoming = jnp.zeros(folded.shape[:3] + (RD, CD), folded.dtype)
    incoming = incoming.at[..., :OV, :].add(tile_shift(folded[..., extended_rows - OV:, OV:OV + CD], 1, 0))
    incoming = incoming.at[..., RD - OV:, :].add(tile_shift(folded[..., :OV, OV:OV + CD], -1, 0))
    incoming = incoming.at[..., :, :OV].add(tile_shift(folded[..., OV:OV + RD, ext_cols - OV:], 0, 1))
    incoming = incoming.at[..., :, CD - OV:].add(tile_shift(folded[..., OV:OV + RD, :OV], 0, -1))
    incoming = incoming.at[..., :OV, :OV].add(tile_shift(folded[..., extended_rows - OV:, ext_cols - OV:], 1, 1))
    incoming = incoming.at[..., :OV, CD - OV:].add(tile_shift(folded[..., extended_rows - OV:, :OV], 1, -1))
    incoming = incoming.at[..., RD - OV:, :OV].add(tile_shift(folded[..., :OV, ext_cols - OV:], -1, 1))
    incoming = incoming.at[..., RD - OV:, CD - OV:].add(tile_shift(folded[..., :OV, :OV], -1, -1))
    return incoming


def globalize(tiles_array):
    planes = tiles_array.shape[2]
    return jnp.transpose(tiles_array, (2, 0, 3, 1, 4)).reshape(planes, N_GY * RD, N_GX * CD)


def reference(prev_wave, source, start_state, storage, leakage, cond_east, cond_south, owner_weight, aggregate, coarse_inverse):
    steps_count, rows_all, cols_all = prev_wave.shape
    col_ids = lax.broadcasted_iota(jnp.int32, (rows_all, cols_all), 1)
    row_ids = lax.broadcasted_iota(jnp.int32, (rows_all, cols_all), 0)
    east = jnp.where(col_ids < cols_all - 1, cond_east, jnp.zeros_like(cond_east))
    south = jnp.where(row_ids < rows_all - 1, cond_south, jnp.zeros_like(cond_south))
    stack = jnp.concatenate([prev_wave, source, start_state[None], storage[None], leakage[None],
                             east[None], south[None], jnp.ones_like(storage)[None]], 0)
    cycle = OV + 1
    padded = jnp.pad(stack, ((0, 0), (cycle, cycle), (cycle, cycle)))

    def one_tile(tile):
        tile_row = (tile // N_GX).astype(jnp.int32)
        tile_col = (tile % N_GX).astype(jnp.int32)
        window = lax.dynamic_slice(padded, (jnp.int32(0), tile_row * RD, tile_col * CD),
                                   (2 * steps_count + 6, RD + 2 * cycle, CD + 2 * cycle))
        return local_sweep(window, steps_count)

    waves = lax.map(one_tile, jnp.arange(N_GY * N_GX, dtype=jnp.int32))
    waves = waves.reshape((N_GY, N_GX) + waves.shape[1:])
    counts_src = jnp.ones((N_GY, N_GX, 1, RD + 2 * OV, CD + 2 * OV), jnp.float32)
    incoming = globalize(gather_rims(waves))
    copies = globalize(gather_rims(counts_src))[0]
    own = globalize(waves[..., OV:OV + RD, OV:OV + CD])
    weight = owner_weight.astype(jnp.float32)
    settled = (weight * own + incoming) / (weight + copies)
    upad = jnp.pad(settled, ((0, 0), (1, 1), (1, 1)))
    east_west = jnp.pad(east, ((0, 0), (1, 0)))[:, :-1]
    south_north = jnp.pad(south, ((1, 0), (0, 0)))[:-1]
    diagonal_entries = storage + leakage + east + east_west + south + south_north
    image = (diagonal_entries * settled - east * upad[:, 1:-1, 2:] - east_west * upad[:, 1:-1, :-2]
             - south * upad[:, 2:, 1:-1] - south_north * upad[:, :-2, 1:-1])
    before = jnp.concatenate([start_state[None], settled[:-1]], 0)
    resid = source + storage * before - image
    coarse = jax.ops.segment_sum(resid.reshape(steps_count, -1).T, aggregate.reshape(-1), num_segments=GROUP_COUNT)
    correction = jnp.dot(coarse_inverse, coarse, precision=lax.Precision.HIGHEST, preferred_element_type=jnp.float32)
    prolonged = jnp.take(correction.T, aggregate, axis=1)
    return settled + prolonged
```

```python
import functools
import math

import jax
import jax.numpy as jnp
import numpy as np
from jax import lax
from jax.experimental import pallas as pl
from jax.experimental.pallas import tpu as pltpu
from jax.sharding import PartitionSpec as P

DEG = 8
OV = 2
STRIDE = 9
LANES = 128
SUB = 8


cheb_theta = 1.0
cheb_delta = 0.95


def horner_coefficients():
    t8 = np.array([1.0, -32.0, 160.0, -256.0, 128.0])
    u_scale = 1.0 / cheb_delta**2
    at_one = sum(c * u_scale**k for k, c in enumerate(t8))
    g = -np.array([c * u_scale**k for k, c in enumerate(t8)]) / at_one
    g[0] += 1.0
    q = np.zeros(4)
    total = 0.0
    for k in range(4):
        total += g[k]
        q[k] = total
    return q


Q_COEF = horner_coefficients()


def lane_ids():
    return lax.broadcasted_iota(jnp.int32, (SUB, LANES), 1)


def row_ids_of(j):
    return lax.broadcasted_iota(jnp.int32, (SUB, LANES), 0) * STRIDE + j


def east_of(x):
    return pltpu.roll(x, LANES - 1, 1)


def west_of(x):
    return pltpu.roll(x, 1, 1)


def south_list(xs):
    return xs[1:] + [pltpu.roll(xs[0], SUB - 1, 0)]


def north_list(xs):
    return [pltpu.roll(xs[-1], 1, 0)] + xs[:-1]


def off_diagonal(xs, east, south):
    from_north = north_list([s * x for s, x in zip(south, xs)])
    from_south = [s * x for s, x in zip(south, south_list(xs))]
    out = []
    for j, x in enumerate(xs):
        out.append((west_of(east[j] * x) + east[j] * east_of(x)) + (from_north[j] + from_south[j]))
    return out


def padded_2(block, sides, width):
    for axis, dim in sides:
        count = lax.axis_size(axis)
        forward = [(i, i + 1) for i in range(count - 1)]
        backward = [(target, source) for source, target in forward]
        low = lax.ppermute(
            lax.slice_in_dim(block, block.shape[dim] - width, None, axis=dim), axis, forward
        )
        high = lax.ppermute(lax.slice_in_dim(block, 0, width, axis=dim), axis, backward)
        block = jnp.concatenate([low, block, high], axis=dim)
    return block


def windows_of(left, right, halo_left, halo_right, lanes):
    return (
        jnp.where(lanes < LANES - 3, left, halo_left),
        jnp.where(lanes < LANES // 2, right, left),
        jnp.where(lanes < 3, halo_right, right),
    )


def sweep_kernel(pT, sT, cT, pX, sX, cX, out, rims, coef, carry):
    step0 = pl.program_id(0)
    block_steps = pT.shape[0]
    lanes = lane_ids()
    rows = lambda j: pl.ds(j, SUB, stride=STRIDE)

    def window_set(j, tile_left, tile_right, xref, slot):
        left = pltpu.roll(xref[0, rows(j), :], (2 * LANES - 3 - 4 * slot) % LANES, 1)
        right = pltpu.roll(xref[1, rows(j), :], (2 * LANES - 4 * slot) % LANES, 1)
        return windows_of(tile_left, tile_right, left, right, lanes)

    breaks = (LANES - 4, LANES // 2 - 1, 2)
    outer = (LANES - 3, -1, 2)

    @pl.when(step0 == 0)
    def _():
        planes = [[window_set(j, cT[p, 0, rows(j), :], cT[p, 1, rows(j), :], cX, p) for j in range(STRIDE)] for p in range(5)]
        for w in range(3):
            start, storage, leakage, east, south = [[planes[p][j][w] for j in range(STRIDE)] for p in range(5)]
            east = [jnp.where(lanes == breaks[w], 0.0, e) for e in east]
            north = north_list(south)
            diag, scale = [], []
            for j in range(STRIDE):
                d = storage[j] + leakage[j] + east[j] + west_of(east[j]) + south[j] + north[j]
                row = row_ids_of(j)
                inner = ((row < 66) | (row > 69)) & (lanes != outer[w]) & (d > 0.0)
                diag.append(d)
                scale.append(jnp.where(inner, 1.0 / jnp.sqrt(jnp.where(inner, d, 1.0)), 0.0))
            scale_south = south_list(scale)
            for j in range(STRIDE):
                carry[w, j] = start[j]
                coef[0, w, j] = east[j] * scale[j] * east_of(scale[j])
                coef[1, w, j] = south[j] * scale[j] * scale_south[j]
                coef[2, w, j] = storage[j]
                coef[3, w, j] = diag[j]
                coef[4, w, j] = east[j]
                coef[5, w, j] = south[j]
                coef[6, w, j] = scale[j]
                coef[7, w, j] = scale[j] * np.float32(Q_COEF[3])
        for side in range(2):
            rims[side] = jnp.zeros_like(rims[side])

    def step(i, _):
        t = step0 * block_steps + i
        prev = [window_set(j, pT[i, 0, rows(j), :], pT[i, 1, rows(j), :], pX, t) for j in range(STRIDE)]
        srcs = [window_set(j, sT[i, 0, rows(j), :], sT[i, 1, rows(j), :], sX, t) for j in range(STRIDE)]
        result = []
        for w in range(3):
            x0 = [prev[j][w] for j in range(STRIDE)]
            full = off_diagonal(x0, [coef[4, w, j] for j in range(STRIDE)], [coef[5, w, j] for j in range(STRIDE)])
            z = [
                coef[6, w, j] * ((srcs[j][w] + coef[2, w, j] * carry[w, j]) + (full[j] - coef[3, w, j] * x0[j]))
                for j in range(STRIDE)
            ]
            east = [coef[0, w, j] for j in range(STRIDE)]
            south = [coef[1, w, j] for j in range(STRIDE)]
            base = [a + b for a, b in zip(z, off_diagonal(z, east, south))]
            y = base
            for k in (2, 1, 0):
                y = off_diagonal(off_diagonal(y, east, south), east, south)
                ratio = np.float32(Q_COEF[k] / Q_COEF[3])
                y = [a + ratio * b for a, b in zip(y, base)]
            result.append([x0[j] + coef[7, w, j] * y[j] for j in range(STRIDE)])
        for j in range(STRIDE):
            a, b, c = result[0][j], result[1][j], result[2][j]
            left = jnp.where(lanes < 96, a, b)
            right = jnp.where(lanes < 32, b, c)
            out[i, 0, rows(j), :] = left
            out[i, 1, rows(j), :] = right
            fresh = windows_of(left, right, a, c, lanes)
            for w in range(3):
                carry[w, j] = fresh[w]
            slot = 4 * t
            here = (lanes >= slot) & (lanes < slot + 3)
            rims[0, rows(j), :] = jnp.where(here, pltpu.roll(a, (slot + 2) % LANES, 1), rims[0, rows(j), :])
            rims[1, rows(j), :] = jnp.where(here, pltpu.roll(c, (slot + 1) % LANES, 1), rims[1, rows(j), :])
        return 0

    lax.fori_loop(0, block_steps, step, 0)


def sweep(pT, sT, cT, pX, sX, cX):
    steps = pT.shape[0]
    block = 4
    rows = pT.shape[2]
    big = pl.BlockSpec((block, 2, rows, LANES), lambda i: (i, 0, 0, 0))
    const = lambda a: pl.BlockSpec(a.shape, lambda i: (0,) * a.ndim)
    return pl.pallas_call(
        sweep_kernel,
        grid=(steps // block,),
        in_specs=[big, big, const(cT), const(pX), const(sX), const(cX)],
        out_specs=[big, pl.BlockSpec((2, rows, LANES), lambda i: (0, 0, 0))],
        out_shape=[jax.ShapeDtypeStruct(pT.shape, jnp.float32), jax.ShapeDtypeStruct((2, rows, LANES), jnp.float32)],
        scratch_shapes=[pltpu.VMEM((8, 3, STRIDE, SUB, LANES), jnp.float32), pltpu.VMEM((3, STRIDE, SUB, LANES), jnp.float32)],
        compiler_params=pltpu.CompilerParams(vmem_limit_bytes=48 * 1024 * 1024),
        name="sweep",
    )(pT, sT, cT, pX, sX, cX)


def circular(x):
    pad = jnp.zeros(x.shape[:-2] + (2,) + x.shape[-1:], x.dtype)
    return jnp.concatenate([x[..., 3:, :], pad, x[..., :3, :]], axis=-2)


def tiles_and_sides(x):
    x = circular(x)
    tiles = jnp.stack([x[..., 3:131], x[..., 131:259]], 1)
    sides = []
    for s in (x[..., 0:3], x[..., 259:262]):
        s = jnp.pad(s, ((0, 32 - s.shape[0]), (0, 0), (0, 1)))
        sides.append(jnp.transpose(s, (1, 0, 2)).reshape(72, LANES))
    return tiles, jnp.stack(sides)


def local_sweep(stack, steps_count):
    pT, pX = tiles_and_sides(stack[:steps_count])
    sT, sX = tiles_and_sides(stack[steps_count : 2 * steps_count])
    cT, cX = tiles_and_sides(stack[2 * steps_count : 2 * steps_count + 5])
    out, rims = sweep(pT, sT, cT, pX, sX, cX)
    rims = jnp.transpose(rims.reshape(2, 72, 32, 4), (0, 2, 1, 3))
    full = jnp.concatenate([rims[0, :, :, 0:2], out[:, 0], out[:, 1], rims[1, :, :, 1:3]], axis=-1)
    return jnp.concatenate([full[:, 70:72], full[:, :66]], axis=1)


def collect_rims(returned, rows_dev, cols_dev):
    lower = rows_dev + 3 * OV
    rightmost = cols_dev + 3 * OV
    incoming = jnp.zeros((returned.shape[0], rows_dev, cols_dev), returned.dtype)
    incoming = incoming.at[:, :OV, :].add(returned[:, :OV, 2 * OV : 2 * OV + cols_dev])
    incoming = incoming.at[:, rows_dev - OV :, :].add(
        returned[:, lower:, 2 * OV : 2 * OV + cols_dev]
    )
    incoming = incoming.at[:, :, :OV].add(returned[:, 2 * OV : 2 * OV + rows_dev, :OV])
    incoming = incoming.at[:, :, cols_dev - OV :].add(
        returned[:, 2 * OV : 2 * OV + rows_dev, rightmost:]
    )
    incoming = incoming.at[:, :OV, :OV].add(returned[:, :OV, :OV])
    incoming = incoming.at[:, :OV, cols_dev - OV :].add(returned[:, :OV, rightmost:])
    incoming = incoming.at[:, rows_dev - OV :, :OV].add(returned[:, lower:, :OV])
    incoming = incoming.at[:, rows_dev - OV :, cols_dev - OV :].add(returned[:, lower:, rightmost:])
    return incoming


def gather_all(own):
    count = lax.axis_size("gx") * lax.axis_size("gy")
    block = own.reshape(1, 1, own.size)
    every = lax.all_to_all(
        jnp.broadcast_to(block, (count,) + block.shape[1:]), ("gx", "gy"), 0, 0
    )
    return every.reshape(count * own.shape[0], own.shape[1])


def shards(
    prev_wave,
    source,
    start_state,
    storage,
    leakage,
    cond_east,
    cond_south,
    owner_weight,
    aggregate,
    coarse_inverse,
):
    steps_count, rows_dev, cols_dev = prev_wave.shape
    rows_all = rows_dev * lax.axis_size("gy")
    cols_all = cols_dev * lax.axis_size("gx")
    col_ids = lax.axis_index("gx") * cols_dev + lax.broadcasted_iota(
        jnp.int32, (rows_dev, cols_dev), 1
    )
    row_ids = lax.axis_index("gy") * rows_dev + lax.broadcasted_iota(
        jnp.int32, (rows_dev, cols_dev), 0
    )
    east = jnp.where(col_ids < cols_all - 1, cond_east, jnp.zeros_like(cond_east))
    south = jnp.where(row_ids < rows_all - 1, cond_south, jnp.zeros_like(cond_south))
    cycle = OV + 1
    stack = jnp.concatenate(
        [
            prev_wave,
            source,
            start_state[None],
            storage[None],
            leakage[None],
            east[None],
            south[None],
            jnp.ones_like(storage)[None],
        ],
        0,
    )
    padded = padded_2(stack, (("gx", 2), ("gy", 1)), cycle)
    waves = local_sweep(padded, steps_count)
    folded = jnp.concatenate([waves, jnp.ones_like(waves[:1])], 0)
    returned = padded_2(folded, (("gx", 2), ("gy", 1)), OV)
    incoming = collect_rims(returned, rows_dev, cols_dev)
    own = waves[:, OV : OV + rows_dev, OV : OV + cols_dev]
    weight = owner_weight.astype(jnp.float32)
    settled = (weight * own + incoming[:steps_count]) / (weight + incoming[steps_count])
    upad = padded_2(settled, (("gx", 2), ("gy", 1)), 1)
    east_west = padded[
        2 * steps_count + 3, cycle : cycle + rows_dev, cycle - 1 : cycle - 1 + cols_dev
    ]
    south_north = padded[
        2 * steps_count + 4, cycle - 1 : cycle - 1 + rows_dev, cycle : cycle + cols_dev
    ]
    diagonal_entries = storage + leakage + east + east_west + south + south_north
    image = (
        diagonal_entries * settled
        - east * upad[:, 1:-1, 2:]
        - east_west * upad[:, 1:-1, :-2]
        - south * upad[:, 2:, 1:-1]
        - south_north * upad[:, :-2, 1:-1]
    )
    before = jnp.concatenate([start_state[None], settled[:-1]], 0)
    resid = source + storage * before - image
    own_aggs = coarse_inverse.shape[0]
    tile_number = lax.axis_index("gx") * lax.axis_size("gy") + lax.axis_index("gy")
    local_ids = aggregate.reshape(-1) - tile_number * own_aggs
    one_hot = jnp.where(
        local_ids[:, None] == lax.broadcasted_iota(jnp.int32, (1, own_aggs), 1),
        jnp.float32(1.0),
        jnp.float32(0.0),
    )
    own_coarse = lax.dot_general(
        one_hot,
        resid.reshape(steps_count, -1),
        (((0,), (1,)), ((), ())),
        precision=lax.Precision.HIGHEST,
        preferred_element_type=jnp.float32,
    )
    correction = jnp.dot(
        coarse_inverse,
        gather_all(own_coarse),
        precision=lax.Precision.HIGHEST,
        preferred_element_type=jnp.float32,
    )
    prolonged = jnp.dot(
        one_hot, correction, precision=lax.Precision.HIGHEST, preferred_element_type=jnp.float32
    )
    return settled + prolonged.T.reshape(steps_count, rows_dev, cols_dev)


def solution(mesh):
    return jax.shard_map(
        shards,
        mesh=mesh,
        in_specs=(
            P(None, "gy", "gx"),
            P(None, "gy", "gx"),
            P("gy", "gx"),
            P("gy", "gx"),
            P("gy", "gx"),
            P("gy", "gx"),
            P("gy", "gx"),
            P("gy", "gx"),
            P("gy", "gx"),
            P(("gx", "gy"), None),
        ),
        out_specs=P(None, "gy", "gx"),
        check_vma=False,
    )
```

```python
import functools
import math

import jax
import jax.numpy as jnp
import numpy as np
from jax import lax
from jax.experimental import pallas as pl
from jax.experimental.pallas import tpu as pltpu
from jax.sharding import PartitionSpec as P

DEG = 8
OV = 2
STRIDE = 9
LANES = 128
SUB = 8


cheb_theta = 1.0
cheb_delta = 0.95


def horner_coefficients():
    t8 = np.array([1.0, -32.0, 160.0, -256.0, 128.0])
    u_scale = 1.0 / cheb_delta**2
    at_one = sum(c * u_scale**k for k, c in enumerate(t8))
    g = -np.array([c * u_scale**k for k, c in enumerate(t8)]) / at_one
    g[0] += 1.0
    q = np.zeros(4)
    total = 0.0
    for k in range(4):
        total += g[k]
        q[k] = total
    return q


Q_COEF = horner_coefficients()


def sub_ids():
    return lax.broadcasted_iota(jnp.int32, (SUB, LANES), 0)


def lane_ids():
    return lax.broadcasted_iota(jnp.int32, (SUB, LANES), 1)


def row_ids_of(j):
    return lax.broadcasted_iota(jnp.int32, (SUB, LANES), 0) * STRIDE + j


def east_of(x):
    return pltpu.roll(x, LANES - 1, 1)


def west_of(x):
    return pltpu.roll(x, 1, 1)


def south_list(xs):
    return xs[1:] + [pltpu.roll(xs[0], SUB - 1, 0)]


def north_list(xs):
    return [pltpu.roll(xs[-1], 1, 0)] + xs[:-1]


def off_diagonal(xs, east, south):
    from_north = north_list([s * x for s, x in zip(south, xs)])
    from_south = [s * x for s, x in zip(south, south_list(xs))]
    out = []
    for j, x in enumerate(xs):
        out.append((west_of(east[j] * x) + east[j] * east_of(x)) + (from_north[j] + from_south[j]))
    return out


GROUPS = 9
PLANES = 6
MIB = 1024 * 1024
START, STORAGE, LEAKAGE, EAST, SOUTH, WEIGHT = range(PLANES)


def tile_of(k):
    return slice(k * LANES, (k + 1) * LANES)


def rows_of(g):
    return slice(g * SUB, (g + 1) * SUB)


def rows(j):
    return pl.ds(j, SUB, stride=STRIDE)


def rolled(x, amount):
    return pltpu.roll(x, lax.rem(amount + 4 * LANES, LANES), 1)


def half_turn(x):
    return pltpu.roll(x, SUB // 2, 0)


def whole(shape):
    return pl.BlockSpec(shape, lambda i: (0,) * len(shape))


def pack_kernel(flags, prev, source, start, storage, leakage, east, south, weight, coef, to_left, to_right, to_up, to_down):
    step0 = pl.program_id(0)
    steps = prev.shape[0]
    total = steps * pl.num_programs(0)
    lanes, sub = lane_ids(), sub_ids()

    def sides(array, slot, get):
        here = (lanes >= slot) & (lanes < slot + 3)
        for g in range(SUB):
            to_left[array, rows_of(g), :] = jnp.where(here, rolled(get(g, 0), slot), to_left[array, rows_of(g), :])
            to_right[array, rows_of(g), :] = jnp.where(here, rolled(get(g, 1), slot + 3), to_right[array, rows_of(g), :])

    def slabs(slab, get_even, get_odd):
        for k in range(2):
            to_up[slab, :, tile_of(k)] = jnp.where(sub < 4, get_even(0, k), half_turn(get_odd(0, k)))
            to_down[slab, :, tile_of(k)] = jnp.where(sub < 4, half_turn(get_odd(SUB - 1, k)), get_even(SUB - 1, k))

    @pl.when(step0 == 0)
    def _():
        for array in range(3):
            to_left[array] = jnp.zeros_like(to_left[array])
            to_right[array] = jnp.zeros_like(to_right[array])
        for p, ref in enumerate((start, storage, leakage, east, south, weight)):
            for g in range(SUB):
                for k in range(2):
                    value = ref[rows_of(g), tile_of(k)].astype(jnp.float32)
                    if p == EAST and k == 1:
                        value = jnp.where((lanes == LANES - 1) & (flags[1] == 0), 0.0, value)
                    if p == SOUTH and g == SUB - 1:
                        value = jnp.where((sub == SUB - 1) & (flags[3] == 0), 0.0, value)
                    coef[p, rows_of(g), tile_of(k)] = value
        plane = lambda p: lambda g, k: coef[p, rows_of(g), tile_of(k)]
        for p in range(PLANES):
            sides(2, 4 * p, plane(p))
        for q in range(PLANES // 2):
            slabs(total + q, plane(2 * q), plane(2 * q + 1))

    def pair(q, _):
        for array, ref in ((0, prev), (1, source)):
            plane = lambda i: lambda g, k: ref[i, rows_of(g), tile_of(k)]
            for o in range(2):
                sides(array, 4 * (step0 * steps + 2 * q + o), plane(2 * q + o))
            slabs(array * (total // 2) + step0 * (steps // 2) + q, plane(2 * q), plane(2 * q + 1))
        return 0

    lax.fori_loop(0, steps // 2, pair, 0)


def pack(flags, prev, source, planes):
    steps, nr, nc = prev.shape
    block = 8
    big = pl.BlockSpec((block, nr, nc), lambda i: (i, 0, 0))
    shapes = [(PLANES, nr, nc), (3, nr, LANES), (3, nr, LANES), (steps + PLANES // 2, SUB, nc), (steps + PLANES // 2, SUB, nc)]
    return pl.pallas_call(
        pack_kernel,
        grid=(steps // block,),
        in_specs=[pl.BlockSpec(memory_space=pltpu.SMEM), big, big] + [whole((nr, nc))] * PLANES,
        out_specs=[whole(s) for s in shapes],
        out_shape=[jax.ShapeDtypeStruct(s, jnp.float32) for s in shapes],
        compiler_params=pltpu.CompilerParams(vmem_limit_bytes=16 * MIB),
        name="pack",
    )(flags, prev, source, *planes)


def windows_of(left, right, halo_left, halo_right, lanes):
    return (
        jnp.where(lanes < LANES - 3, left, halo_left),
        jnp.where(lanes < LANES // 2, right, left),
        jnp.where(lanes < 3, halo_right, right),
    )


def halo_rows(below, above, odd, sub):
    if odd:
        return half_turn(jnp.where(sub < 4, above, below))
    return jnp.where(sub < 4, below, above)


def sweep_kernel(prev, source, coefs, xL, xR, cA, cB, yA, yB, out, rims, yU, yD, tiles, ctiles, halo, coef, carry):
    step0 = pl.program_id(0)
    steps = prev.shape[0]
    total = steps * pl.num_programs(0)
    lanes, sub = lane_ids(), sub_ids()

    def window_set(j, left, right, array, slot):
        return windows_of(
            left, right, rolled(halo[0, array, rows(j), :], LANES - 3 - slot), rolled(halo[1, array, rows(j), :], -slot), lanes
        )

    breaks = (LANES - 4, LANES // 2 - 1, 2)
    outer = (LANES - 3, -1, 2)

    @pl.when(step0 == 0)
    def _():
        for array in range(3):
            for side, ref in ((0, xL), (1, xR)):
                for g in range(SUB):
                    halo[side, array, rows_of(g), :] = ref[array, rows_of(g), :]
                halo[side, array, rows_of(SUB), :] = jnp.where(sub < 4, cB[side, array], cA[side, array])
        for p in range(5):
            slab = total + p // 2
            for k in range(2):
                for g in range(SUB):
                    ctiles[p, k, rows_of(g), :] = coefs[p, rows_of(g), tile_of(k)]
                ctiles[p, k, rows_of(SUB), :] = halo_rows(yB[slab, :, tile_of(k)], yA[slab, :, tile_of(k)], p % 2, sub)
        planes = [
            [window_set(j, ctiles[p, 0, rows(j), :], ctiles[p, 1, rows(j), :], 2, 4 * p) for j in range(STRIDE)]
            for p in range(5)
        ]
        for w in range(3):
            start, storage, leakage, east, south = [[planes[p][j][w] for j in range(STRIDE)] for p in range(5)]
            east = [jnp.where(lanes == breaks[w], 0.0, e) for e in east]
            north = north_list(south)
            diag, scale = [], []
            for j in range(STRIDE):
                d = storage[j] + leakage[j] + east[j] + west_of(east[j]) + south[j] + north[j]
                row = row_ids_of(j)
                inner = ((row < 66) | (row > 69)) & (lanes != outer[w]) & (d > 0.0)
                diag.append(d)
                scale.append(jnp.where(inner, 1.0 / jnp.sqrt(jnp.where(inner, d, 1.0)), 0.0))
            scale_south = south_list(scale)
            for j in range(STRIDE):
                carry[w, j] = start[j]
                coef[0, w, j] = east[j] * scale[j] * east_of(scale[j])
                coef[1, w, j] = south[j] * scale[j] * scale_south[j]
                coef[2, w, j] = storage[j]
                coef[3, w, j] = diag[j]
                coef[4, w, j] = east[j]
                coef[5, w, j] = south[j]
                coef[6, w, j] = scale[j]
                coef[7, w, j] = scale[j] * np.float32(Q_COEF[3])
        for side in range(2):
            rims[side] = jnp.zeros_like(rims[side])

    def step(i, t, odd):
        for array, ref in ((0, prev), (1, source)):
            slab = array * (total // 2) + t // 2
            for k in range(2):
                for g in range(SUB):
                    tiles[odd, array, k, rows_of(g), :] = ref[i, rows_of(g), tile_of(k)]
                tiles[odd, array, k, rows_of(SUB), :] = halo_rows(yB[slab, :, tile_of(k)], yA[slab, :, tile_of(k)], odd, sub)
        x0s, srcs = [
            [window_set(j, tiles[odd, a, 0, rows(j), :], tiles[odd, a, 1, rows(j), :], a, 4 * t) for j in range(STRIDE)]
            for a in range(2)
        ]
        result = []
        for w in range(3):
            x0 = [x0s[j][w] for j in range(STRIDE)]
            full = off_diagonal(x0, [coef[4, w, j] for j in range(STRIDE)], [coef[5, w, j] for j in range(STRIDE)])
            z = [
                coef[6, w, j] * ((srcs[j][w] + coef[2, w, j] * carry[w, j]) + (full[j] - coef[3, w, j] * x0[j]))
                for j in range(STRIDE)
            ]
            east = [coef[0, w, j] for j in range(STRIDE)]
            south = [coef[1, w, j] for j in range(STRIDE)]
            base = [a + b for a, b in zip(z, off_diagonal(z, east, south))]
            y = base
            for k in (2, 1, 0):
                y = off_diagonal(off_diagonal(y, east, south), east, south)
                ratio = np.float32(Q_COEF[k] / Q_COEF[3])
                y = [a + ratio * b for a, b in zip(y, base)]
            result.append([x0[j] + coef[7, w, j] * y[j] for j in range(STRIDE)])
        slot = 4 * t
        here = (lanes >= slot) & (lanes < slot + 3)
        for j in range(STRIDE):
            a, b, c = result[0][j], result[1][j], result[2][j]
            left = jnp.where(lanes < 96, a, b)
            right = jnp.where(lanes < 32, b, c)
            out[i, 0, rows(j), :] = left
            out[i, 1, rows(j), :] = right
            fresh = windows_of(left, right, a, c, lanes)
            for w in range(3):
                carry[w, j] = fresh[w]
            rims[0, rows(j), :] = jnp.where(here, rolled(a, slot + 2), rims[0, rows(j), :])
            rims[1, rows(j), :] = jnp.where(here, rolled(c, slot + 1), rims[1, rows(j), :])

    def pair(q, _):
        for odd in range(2):
            step(2 * q + odd, step0 * steps + 2 * q + odd, odd)
        kept = (sub < 2) | (sub > 5)
        slab = step0 * (steps // 2) + q
        for k in range(2):
            down, up = [], []
            for odd in range(2):
                first, last, beyond = [out[2 * q + odd, k, rows_of(g), :] for g in (0, SUB - 1, SUB)]
                down.append(jnp.where(sub < 4, beyond, last))
                up.append(jnp.where(sub < 4, first, beyond))
            yD[slab, :, tile_of(k)] = jnp.where(kept, down[0], half_turn(down[1]))
            yU[slab, :, tile_of(k)] = jnp.where(kept, up[0], half_turn(up[1]))
        return 0

    lax.fori_loop(0, steps // 2, pair, 0)

    @pl.when(step0 == pl.num_programs(0) - 1)
    def _():
        for side in range(2):
            first, last, beyond = [rims[side, rows_of(g), :] for g in (0, SUB - 1, SUB)]
            yD[total // 2, :, tile_of(side)] = jnp.where(sub < 4, beyond, last)
            yU[total // 2, :, tile_of(side)] = jnp.where(sub < 4, first, beyond)


def sweep(prev, source, coefs, xL, xR, cA, cB, yA, yB):
    steps, nr, nc = prev.shape
    block = 4
    big = pl.BlockSpec((block, nr, nc), lambda i: (i, 0, 0))
    ext = GROUPS * SUB
    consts = (coefs, xL, xR, cA, cB, yA, yB)
    rest = [(2, ext, LANES), (steps // 2 + 1, SUB, nc), (steps // 2 + 1, SUB, nc)]
    return pl.pallas_call(
        sweep_kernel,
        grid=(steps // block,),
        in_specs=[big, big] + [whole(a.shape) for a in consts],
        out_specs=[pl.BlockSpec((block, 2, ext, LANES), lambda i: (i, 0, 0, 0))] + [whole(s) for s in rest],
        out_shape=[jax.ShapeDtypeStruct(s, jnp.float32) for s in [(steps, 2, ext, LANES)] + rest],
        scratch_shapes=[
            pltpu.VMEM((2, 2, 2, ext, LANES), jnp.float32),
            pltpu.VMEM((5, 2, ext, LANES), jnp.float32),
            pltpu.VMEM((2, 3, ext, LANES), jnp.float32),
            pltpu.VMEM((8, 3, STRIDE, SUB, LANES), jnp.float32),
            pltpu.VMEM((3, STRIDE, SUB, LANES), jnp.float32),
        ],
        compiler_params=pltpu.CompilerParams(vmem_limit_bytes=16 * MIB),
        name="sweep",
    )(prev, source, *consts)


def split3(x):
    hi = x.astype(jnp.bfloat16)
    left = x - hi.astype(jnp.float32)
    mid = left.astype(jnp.bfloat16)
    low = (left - mid.astype(jnp.float32)).astype(jnp.bfloat16)
    return hi, mid, low


def settle_kernel(
    flags, local, source, coefs, xL, xR, yA, yB, rims, rL, rR, kA, kB, sA, sB, ids, settled, coarse, pack, ring, edge, before, resid
):
    step0 = pl.program_id(0)
    steps = local.shape[0]
    total = steps * pl.num_programs(0)
    lanes, sub = lane_ids(), sub_ids()
    has_left, has_right, has_up, has_down = [(flags[k] != 0) for k in range(4)]
    as_one = lambda mask: jnp.where(mask, 1.0, 0.0)
    only = lambda mask, x: jnp.where(mask, x, 0.0)

    def column(ref, g, lane):
        return jnp.broadcast_to(ref[2, rows_of(g), lane : lane + 1], (SUB, LANES))

    def halo_plane(p, k):
        slab = total + p // 2
        return halo_rows(yB[slab, :, tile_of(k)], yA[slab, :, tile_of(k)], p % 2, sub)

    @pl.when(step0 == 0)
    def _():
        across = lambda k: as_one((lanes < 2) & has_left) if k == 0 else as_one((lanes > LANES - 3) & has_right)
        for g in range(GROUPS):
            if g < SUB:
                down = only(sub < 2, as_one(has_up)) if g == 0 else only(sub > 5, as_one(has_down)) if g == SUB - 1 else 0.0 * as_one(sub < 0)
            else:
                down = as_one(sub >= 0)
            for k in range(2):
                copies = (1.0 + across(k)) * (1.0 + down) - 1.0
                weight = coefs[WEIGHT, rows_of(g), tile_of(k)] if g < SUB else halo_plane(WEIGHT, k)
                ring[0, k, g] = weight / (weight + copies)
                ring[1, k, g] = 1.0 / (weight + copies)
            for side, got, xref, lane, keep, back in ((0, rL, xL, 4 * WEIGHT + 2, 0, LANES - 1), (1, rR, xR, 4 * WEIGHT, 2, 1)):
                arrived = got[rows_of(g), :]
                fwd_above, fwd_below = sA[:, tile_of(side)], sB[:, tile_of(side)]
                if g == 0:
                    extra = only(sub < 2, fwd_above)
                elif g == SUB - 1:
                    extra = only(sub > 5, fwd_below)
                elif g == SUB:
                    extra = only(sub == SUB - 1, fwd_above) + only(sub == 0, fwd_below)
                else:
                    extra = jnp.zeros((SUB, LANES), jnp.float32)
                value = arrived + extra
                if g < SUB:
                    mine = rims[side, rows_of(g), :]
                    if g == 0:
                        mine = mine + only(sub < 2, kA[total // 2, :, tile_of(side)])
                    if g == SUB - 1:
                        mine = mine + only(sub > 5, kB[total // 2, :, tile_of(side)])
                    weight = column(xref, g, lane)
                    copies = 2.0 * (1.0 + down) - 1.0
                    outer = (weight * arrived + (pltpu.roll(mine, back, 1) + extra)) / (weight + copies)
                    value = jnp.where(lax.rem(lanes, 4) == keep, outer, value)
                edge[side, g] = value
        for k in range(2):
            for g in range(SUB):
                own = lambda p: coefs[p, rows_of(g), tile_of(k)]
                neighbour = column(xL, g, 4 * EAST + 2) if k == 0 else coefs[EAST, rows_of(g), tile_of(0)]
                west = west_of(jnp.where(lanes == LANES - 1, neighbour, own(EAST)))
                above = halo_plane(SOUTH, k) if g == 0 else coefs[SOUTH, rows_of(g - 1), tile_of(k)]
                north = pltpu.roll(jnp.where(sub == SUB - 1, above, own(SOUTH)), 1, 0)
                pack[0, k, g] = west
                pack[1, k, g] = north
                pack[2, k, g] = own(STORAGE) + own(LEAKAGE) + own(EAST) + west + own(SOUTH) + north
                before[k, g] = own(START)

    def step(i, t, odd):
        slab = t // 2
        mid = []
        for k in range(2):
            from_above, from_below = kA[slab, :, tile_of(k)], kB[slab, :, tile_of(k)]
            if odd:
                from_above, from_below = half_turn(from_above), half_turn(from_below)
            values = []
            for g in range(GROUPS):
                side = rolled(edge[k, g], -4 * t - 1 if k == 0 else LANES - 2 - 4 * t)
                extra = only(lanes < 2 if k == 0 else lanes > LANES - 3, side)
                here = local[i, k, rows_of(g), :]
                if g == 0:
                    extra = extra + only(sub < 2, from_above)
                elif g == SUB - 1:
                    extra = extra + only(sub > 5, from_below)
                elif g == SUB:
                    extra = extra + here
                    here = jnp.where(sub < 4, from_below, from_above)
                values.append((ring[0, k, g] * here + ring[1, k, g] * extra, side))
            mid.append(values)
        for k in range(2):
            for g in range(SUB):
                x = mid[k][g][0]
                if k == 0:
                    west = jnp.where(lanes == LANES - 1, mid[0][g][1], x)
                    east = jnp.where(lanes == 0, mid[1][g][0], x)
                else:
                    west = jnp.where(lanes == LANES - 1, mid[0][g][0], x)
                    east = jnp.where(lanes == 0, mid[1][g][1], x)
                north = jnp.where(sub == SUB - 1, mid[k][(g + GROUPS - 1) % GROUPS][0], x)
                south = jnp.where(sub == 0, mid[k][g + 1][0], x)
                around = (coefs[EAST, rows_of(g), tile_of(k)] * east_of(east) + pack[0, k, g] * west_of(west)) + (
                    coefs[SOUTH, rows_of(g), tile_of(k)] * pltpu.roll(south, SUB - 1, 0) + pack[1, k, g] * pltpu.roll(north, 1, 0)
                )
                value = (source[i, rows_of(g), tile_of(k)] + coefs[STORAGE, rows_of(g), tile_of(k)] * before[k, g]) - (
                    pack[2, k, g] * x - around
                )
                resid[k, pl.ds(t * 64 + g * SUB, SUB), :] = value
                before[k, g] = x
                settled[i, rows_of(g), tile_of(k)] = x

    def pair(q, _):
        for odd in range(2):
            step(2 * q + odd, step0 * steps + 2 * q + odd, odd)
        return 0

    lax.fori_loop(0, steps // 2, pair, 0)

    @pl.when(step0 == pl.num_programs(0) - 1)
    def _():
        aggs = lax.broadcasted_iota(jnp.int32, (64, 2 * LANES), 0)

        def one_row(r, acc):
            picked = jnp.broadcast_to(ids[pl.ds(r, 1), :] - flags[4], (64, 2 * LANES))
            hot = jnp.where(picked == aggs, 1.0, 0.0).astype(jnp.bfloat16)
            values = jnp.concatenate([resid[k, pl.ds(r, total, stride=64), :] for k in range(2)], axis=1)
            parts = jnp.concatenate(split3(values), axis=0)
            return acc + lax.dot_general(parts, hot, (((1,), (1,)), ((), ())), preferred_element_type=jnp.float32)

        def rows4(r, acc):
            for o in range(4):
                acc = one_row(4 * r + o, acc)
            return acc

        acc = lax.fori_loop(0, 16, rows4, jnp.zeros((3 * total, 64), jnp.float32))
        sums = acc[:total] + acc[total : 2 * total] + acc[2 * total :]
        block = jnp.concatenate([sums[: total // 2], sums[total // 2 :]], axis=1)
        coarse[...] = jnp.broadcast_to(block[None], coarse.shape)


def settle(flags, local, source, coefs, xL, xR, yA, yB, rims, rL, rR, kA, kB, sA, sB, ids, count):
    steps, nr, nc = source.shape
    block = 4
    ext = GROUPS * SUB
    big = pl.BlockSpec((block, nr, nc), lambda i: (i, 0, 0))
    consts = (coefs, xL, xR, yA, yB, rims, rL, rR, kA, kB, sA, sB, ids)
    shapes = [(steps, nr, nc), (count, steps // 2, LANES)]
    return pl.pallas_call(
        settle_kernel,
        grid=(steps // block,),
        in_specs=[
            pl.BlockSpec(memory_space=pltpu.SMEM),
            pl.BlockSpec((block, 2, ext, LANES), lambda i: (i, 0, 0, 0)),
            big,
        ]
        + [whole(a.shape) for a in consts],
        out_specs=[big, whole(shapes[1])],
        out_shape=[jax.ShapeDtypeStruct(s, jnp.float32) for s in shapes],
        scratch_shapes=[
            pltpu.VMEM((3, 2, SUB, SUB, LANES), jnp.float32),
            pltpu.VMEM((2, 2, GROUPS, SUB, LANES), jnp.float32),
            pltpu.VMEM((2, GROUPS, SUB, LANES), jnp.float32),
            pltpu.VMEM((2, SUB, SUB, LANES), jnp.float32),
            pltpu.VMEM((2, steps * nr, LANES), jnp.float32),
        ],
        compiler_params=pltpu.CompilerParams(vmem_limit_bytes=20 * MIB),
        name="settle",
    )(flags, local, source, *consts)


def finish_kernel(flags, every, inverse, settled, ids, out, table, stacked):
    step0 = pl.program_id(0)
    steps = settled.shape[0]
    half = every.shape[1]
    lanes = lane_ids()

    @pl.when(step0 == 0)
    def _():
        for d in range(every.shape[0] // 2):
            for g in range(half // SUB):
                a, b = every[2 * d, rows_of(g), :], every[2 * d + 1, rows_of(g), :]
                stacked[rows_of(g), tile_of(d)] = jnp.where(lanes < LANES // 2, a, pltpu.roll(b, LANES // 2, 1))
                stacked[half + g * SUB : half + (g + 1) * SUB, tile_of(d)] = jnp.where(
                    lanes < LANES // 2, pltpu.roll(a, LANES // 2, 1), b
                )
        product = lax.dot_general(
            stacked[...],
            inverse[...],
            (((1,), (1,)), ((), ())),
            precision=lax.Precision.HIGHEST,
            preferred_element_type=jnp.float32,
        )
        table[...] = jnp.concatenate([product, product], axis=1)

    def step(i, _):
        t = step0 * steps + i
        row = jnp.broadcast_to(table[pl.ds(t, 1), :], (SUB, LANES))
        for g in range(SUB):
            for k in range(2):
                picked = ids[rows_of(g), tile_of(k)] - flags[4]
                out[i, rows_of(g), tile_of(k)] = settled[i, rows_of(g), tile_of(k)] + jnp.take_along_axis(row, picked, axis=1)
        return 0

    lax.fori_loop(0, steps, step, 0)


def finish(flags, every, inverse, settled, ids):
    steps, nr, nc = settled.shape
    block = 8
    big = pl.BlockSpec((block, nr, nc), lambda i: (i, 0, 0))
    return pl.pallas_call(
        finish_kernel,
        grid=(steps // block,),
        in_specs=[pl.BlockSpec(memory_space=pltpu.SMEM), whole(every.shape), whole(inverse.shape), big, whole(ids.shape)],
        out_specs=big,
        out_shape=jax.ShapeDtypeStruct(settled.shape, jnp.float32),
        scratch_shapes=[pltpu.VMEM((steps, LANES), jnp.float32), pltpu.VMEM((steps, inverse.shape[1]), jnp.float32)],
        compiler_params=pltpu.CompilerParams(vmem_limit_bytes=20 * MIB),
        name="finish",
    )(flags, every, inverse, settled, ids)


def neighbours(low, high, axis):
    count = lax.axis_size(axis)
    forward = [(i, i + 1) for i in range(count - 1)]
    backward = [(target, source) for source, target in forward]
    return lax.ppermute(high, axis, forward), lax.ppermute(low, axis, backward)


def gather_all(block, axes):
    count = block.shape[0]
    every = lax.all_to_all(block.reshape(count, 1, -1), axes, 0, 0)
    return every.reshape(block.shape)


def shards(
    prev_wave,
    source,
    start_state,
    storage,
    leakage,
    cond_east,
    cond_south,
    owner_weight,
    aggregate,
    coarse_inverse,
):
    gx, gy = lax.axis_index("gx"), lax.axis_index("gy")
    nx, ny = lax.axis_size("gx"), lax.axis_size("gy")
    flags = jnp.stack([gx, nx - 1 - gx, gy, ny - 1 - gy, (gx * ny + gy) * coarse_inverse.shape[0]]).astype(jnp.int32)
    planes = (start_state, storage, leakage, cond_east, cond_south, owner_weight)
    coefs, to_left, to_right, to_up, to_down = pack(flags, prev_wave, source, planes)
    xL, xR = neighbours(to_left, to_right, "gx")
    yA, yB = neighbours(to_up, to_down, "gy")
    both = jnp.stack([xL, xR])
    cA, cB = neighbours(both[:, :, :SUB], both[:, :, -SUB:], "gy")
    local, rims, yU, yD = sweep(prev_wave, source, coefs, xL, xR, cA, cB, yA, yB)
    rL, rR = neighbours(rims[0], rims[1], "gx")
    kA, kB = neighbours(yU, yD, "gy")
    up = jnp.concatenate([jnp.concatenate([r[0:4], r[68:72]], 0) for r in (rL, rR)], 1)
    down = jnp.concatenate([jnp.concatenate([r[64:68], r[60:64]], 0) for r in (rL, rR)], 1)
    sA, sB = neighbours(up, down, "gy")
    settled, coarse = settle(
        flags, local, source, coefs, xL, xR, yA, yB, rims, rL, rR, kA, kB, sA, sB, aggregate, nx * ny
    )
    every = gather_all(coarse, ("gx", "gy"))
    return finish(flags, every, coarse_inverse, settled, aggregate)


def solution(mesh):
    return jax.shard_map(
        shards,
        mesh=mesh,
        in_specs=(
            P(None, "gy", "gx"),
            P(None, "gy", "gx"),
            P("gy", "gx"),
            P("gy", "gx"),
            P("gy", "gx"),
            P("gy", "gx"),
            P("gy", "gx"),
            P("gy", "gx"),
            P("gy", "gx"),
            P(("gx", "gy"), None),
        ),
        out_specs=P(None, "gy", "gx"),
        check_vma=False,
    )
```

```python
import functools
import math

import jax
import jax.numpy as jnp
import numpy as np
from jax import lax
from jax.experimental import pallas as pl
from jax.experimental.pallas import tpu as pltpu
from jax.sharding import PartitionSpec as P

DEG = 8
OV = 2
STRIDE = 9
LANES = 128
SUB = 8


cheb_theta = 1.0
cheb_delta = 0.95


def horner_coefficients():
    t8 = np.array([1.0, -32.0, 160.0, -256.0, 128.0])
    u_scale = 1.0 / cheb_delta**2
    at_one = sum(c * u_scale**k for k, c in enumerate(t8))
    g = -np.array([c * u_scale**k for k, c in enumerate(t8)]) / at_one
    g[0] += 1.0
    q = np.zeros(4)
    total = 0.0
    for k in range(4):
        total += g[k]
        q[k] = total
    return q


Q_COEF = horner_coefficients()


def sub_ids():
    return lax.broadcasted_iota(jnp.int32, (SUB, LANES), 0)


def lane_ids():
    return lax.broadcasted_iota(jnp.int32, (SUB, LANES), 1)


def row_ids_of(j):
    return lax.broadcasted_iota(jnp.int32, (SUB, LANES), 0) * STRIDE + j


def east_of(x):
    return pltpu.roll(x, LANES - 1, 1)


def west_of(x):
    return pltpu.roll(x, 1, 1)


def south_list(xs):
    return xs[1:] + [pltpu.roll(xs[0], SUB - 1, 0)]


def north_list(xs):
    return [pltpu.roll(xs[-1], 1, 0)] + xs[:-1]


def off_diagonal(xs, east, south):
    from_north = north_list([s * x for s, x in zip(south, xs)])
    from_south = [s * x for s, x in zip(south, south_list(xs))]
    out = []
    for j, x in enumerate(xs):
        out.append((west_of(east[j] * x) + east[j] * east_of(x)) + (from_north[j] + from_south[j]))
    return out


GROUPS = 9
PLANES = 6
MIB = 1024 * 1024
START, STORAGE, LEAKAGE, EAST, SOUTH, WEIGHT = range(PLANES)


def tile_of(k):
    return slice(k * LANES, (k + 1) * LANES)


def rows_of(g):
    return slice(g * SUB, (g + 1) * SUB)


def rows(j):
    return pl.ds(j, SUB, stride=STRIDE)


def rolled(x, amount):
    return pltpu.roll(x, lax.rem(amount + 4 * LANES, LANES), 1)


def half_turn(x):
    return pltpu.roll(x, SUB // 2, 0)


def whole(shape):
    return pl.BlockSpec(shape, lambda i: (0,) * len(shape))


def pack_kernel(flags, prev, source, start, storage, leakage, east, south, weight, coef, to_left, to_right, to_up, to_down):
    step0 = pl.program_id(0)
    steps = prev.shape[0]
    total = steps * pl.num_programs(0)
    lanes, sub = lane_ids(), sub_ids()

    def sides(array, slot, get):
        here = (lanes >= slot) & (lanes < slot + 3)
        for g in range(SUB):
            to_left[array, rows_of(g), :] = jnp.where(here, rolled(get(g, 0), slot), to_left[array, rows_of(g), :])
            to_right[array, rows_of(g), :] = jnp.where(here, rolled(get(g, 1), slot + 3), to_right[array, rows_of(g), :])

    def slabs(slab, get_even, get_odd):
        for k in range(2):
            to_up[slab, :, tile_of(k)] = jnp.where(sub < 4, get_even(0, k), half_turn(get_odd(0, k)))
            to_down[slab, :, tile_of(k)] = jnp.where(sub < 4, half_turn(get_odd(SUB - 1, k)), get_even(SUB - 1, k))

    @pl.when(step0 == 0)
    def _():
        for array in range(3):
            to_left[array] = jnp.zeros_like(to_left[array])
            to_right[array] = jnp.zeros_like(to_right[array])
        for p, ref in enumerate((start, storage, leakage, east, south, weight)):
            for g in range(SUB):
                for k in range(2):
                    value = ref[rows_of(g), tile_of(k)].astype(jnp.float32)
                    if p == EAST and k == 1:
                        value = jnp.where((lanes == LANES - 1) & (flags[1] == 0), 0.0, value)
                    if p == SOUTH and g == SUB - 1:
                        value = jnp.where((sub == SUB - 1) & (flags[3] == 0), 0.0, value)
                    coef[p, rows_of(g), tile_of(k)] = value
        plane = lambda p: lambda g, k: coef[p, rows_of(g), tile_of(k)]
        for p in range(PLANES):
            sides(2, 4 * p, plane(p))
        for q in range(PLANES // 2):
            slabs(total + q, plane(2 * q), plane(2 * q + 1))

    def pair(q, _):
        for array, ref in ((0, prev), (1, source)):
            plane = lambda i: lambda g, k: ref[i, rows_of(g), tile_of(k)]
            for o in range(2):
                sides(array, 4 * (step0 * steps + 2 * q + o), plane(2 * q + o))
            slabs(array * (total // 2) + step0 * (steps // 2) + q, plane(2 * q), plane(2 * q + 1))
        return 0

    lax.fori_loop(0, steps // 2, pair, 0)


def pack(flags, prev, source, planes):
    steps, nr, nc = prev.shape
    block = 8
    big = pl.BlockSpec((block, nr, nc), lambda i: (i, 0, 0))
    row_slabs = (steps + PLANES // 2 + 3, SUB, nc)
    shapes = [(PLANES, nr, nc), (3, nr, LANES), (3, nr, LANES), row_slabs, row_slabs]
    return pl.pallas_call(
        pack_kernel,
        grid=(steps // block,),
        in_specs=[pl.BlockSpec(memory_space=pltpu.SMEM), big, big] + [whole((nr, nc))] * PLANES,
        out_specs=[whole(s) for s in shapes],
        out_shape=[jax.ShapeDtypeStruct(s, jnp.float32) for s in shapes],
        compiler_params=pltpu.CompilerParams(vmem_limit_bytes=60 * MIB),
        name="pack",
    )(flags, prev, source, *planes)


def windows_of(left, right, halo_left, halo_right, lanes):
    return (
        jnp.where(lanes < LANES - 3, left, halo_left),
        jnp.where(lanes < LANES // 2, right, left),
        jnp.where(lanes < 3, halo_right, right),
    )


def halo_rows(below, above, odd, sub):
    if odd:
        return half_turn(jnp.where(sub < 4, above, below))
    return jnp.where(sub < 4, below, above)


def present(x, flag):
    return jnp.where(flag != 0, x, 0.0)


def sweep_kernel(flags, prev, source, coefs, xL, xR, yA, yB, out, rims, yU, yD, tiles, ctiles, halo, coef, carry):
    step0 = pl.program_id(0)
    steps = prev.shape[0]
    total = steps * pl.num_programs(0)
    lanes, sub = lane_ids(), sub_ids()

    def window_set(j, left, right, array, slot):
        return windows_of(
            left, right, rolled(halo[0, array, rows(j), :], LANES - 3 - slot), rolled(halo[1, array, rows(j), :], -slot), lanes
        )

    breaks = (LANES - 4, LANES // 2 - 1, 2)
    outer = (LANES - 3, -1, 2)

    @pl.when(step0 == 0)
    def _():
        for array in range(3):
            for side, ref in ((0, xL), (1, xR)):
                slab = total + PLANES // 2 + array
                below, above = yB[slab, :, tile_of(side)], yA[slab, :, tile_of(side)]
                if array == 2:
                    below, above = present(below, flags[3]), present(above, flags[2])
                parts = [ref[array, rows_of(g), :] for g in range(SUB)] + [jnp.where(sub < 4, below, above)]
                for g in range(GROUPS):
                    halo[side, array, rows_of(g), :] = present(parts[g], flags[side]) if array == 2 else parts[g]
        for p in range(5):
            slab = total + p // 2
            for k in range(2):
                for g in range(SUB):
                    ctiles[p, k, rows_of(g), :] = coefs[p, rows_of(g), tile_of(k)]
                ctiles[p, k, rows_of(SUB), :] = halo_rows(
                    present(yB[slab, :, tile_of(k)], flags[3]), present(yA[slab, :, tile_of(k)], flags[2]), p % 2, sub
                )
        planes = [
            [window_set(j, ctiles[p, 0, rows(j), :], ctiles[p, 1, rows(j), :], 2, 4 * p) for j in range(STRIDE)]
            for p in range(5)
        ]
        for w in range(3):
            start, storage, leakage, east, south = [[planes[p][j][w] for j in range(STRIDE)] for p in range(5)]
            east = [jnp.where(lanes == breaks[w], 0.0, e) for e in east]
            north = north_list(south)
            diag, scale = [], []
            for j in range(STRIDE):
                d = storage[j] + leakage[j] + east[j] + west_of(east[j]) + south[j] + north[j]
                row = row_ids_of(j)
                inner = ((row < 66) | (row > 69)) & (lanes != outer[w]) & (d > 0.0)
                diag.append(d)
                scale.append(jnp.where(inner, 1.0 / jnp.sqrt(jnp.where(inner, d, 1.0)), 0.0))
            scale_south = south_list(scale)
            for j in range(STRIDE):
                carry[w, j] = start[j]
                coef[0, w, j] = east[j] * scale[j] * east_of(scale[j])
                coef[1, w, j] = south[j] * scale[j] * scale_south[j]
                coef[2, w, j] = storage[j]
                coef[3, w, j] = diag[j]
                coef[4, w, j] = east[j]
                coef[5, w, j] = south[j]
                coef[6, w, j] = scale[j]
                coef[7, w, j] = scale[j] * np.float32(Q_COEF[3])
        for side in range(2):
            rims[side] = jnp.zeros_like(rims[side])

    def step(i, t, odd):
        for array, ref in ((0, prev), (1, source)):
            slab = array * (total // 2) + t // 2
            for k in range(2):
                for g in range(SUB):
                    tiles[odd, array, k, rows_of(g), :] = ref[i, rows_of(g), tile_of(k)]
                tiles[odd, array, k, rows_of(SUB), :] = halo_rows(yB[slab, :, tile_of(k)], yA[slab, :, tile_of(k)], odd, sub)
        x0s, srcs = [
            [window_set(j, tiles[odd, a, 0, rows(j), :], tiles[odd, a, 1, rows(j), :], a, 4 * t) for j in range(STRIDE)]
            for a in range(2)
        ]
        every = range(3)
        x0 = [[x0s[j][w] for j in range(STRIDE)] for w in every]
        table = lambda n, w: [coef[n, w, j] for j in range(STRIDE)]
        full = [off_diagonal(x0[w], table(4, w), table(5, w)) for w in every]
        z = [
            [
                coef[6, w, j] * ((srcs[j][w] + coef[2, w, j] * carry[w, j]) + (full[w][j] - coef[3, w, j] * x0[w][j]))
                for j in range(STRIDE)
            ]
            for w in every
        ]
        apply = lambda v: [off_diagonal(v[w], table(0, w), table(1, w)) for w in every]
        base = [[a + b for a, b in zip(p, q)] for p, q in zip(z, apply(z))]
        y = base
        for k in (2, 1, 0):
            y = apply(apply(y))
            ratio = np.float32(Q_COEF[k] / Q_COEF[3])
            y = [[a + ratio * b for a, b in zip(p, q)] for p, q in zip(y, base)]
        result = [[x0[w][j] + coef[7, w, j] * y[w][j] for j in range(STRIDE)] for w in every]
        slot = 4 * t
        here = (lanes >= slot) & (lanes < slot + 3)
        for j in range(STRIDE):
            a, b, c = result[0][j], result[1][j], result[2][j]
            left = jnp.where(lanes < 96, a, b)
            right = jnp.where(lanes < 32, b, c)
            out[i, 0, rows(j), :] = left
            out[i, 1, rows(j), :] = right
            fresh = windows_of(left, right, a, c, lanes)
            for w in range(3):
                carry[w, j] = fresh[w]
            rims[0, rows(j), :] = jnp.where(here, rolled(a, slot + 2), rims[0, rows(j), :])
            rims[1, rows(j), :] = jnp.where(here, rolled(c, slot + 1), rims[1, rows(j), :])

    def pair(q, _):
        for odd in range(2):
            step(2 * q + odd, step0 * steps + 2 * q + odd, odd)
        kept = (sub < 2) | (sub > 5)
        slab = step0 * (steps // 2) + q
        for k in range(2):
            down, up = [], []
            for odd in range(2):
                first, last, beyond = [out[2 * q + odd, k, rows_of(g), :] for g in (0, SUB - 1, SUB)]
                down.append(jnp.where(sub < 4, beyond, last))
                up.append(jnp.where(sub < 4, first, beyond))
            yD[slab, :, tile_of(k)] = jnp.where(kept, down[0], half_turn(down[1]))
            yU[slab, :, tile_of(k)] = jnp.where(kept, up[0], half_turn(up[1]))
        return 0

    lax.fori_loop(0, steps // 2, pair, 0)

    @pl.when(step0 == pl.num_programs(0) - 1)
    def _():
        for side in range(2):
            first, last, beyond = [rims[side, rows_of(g), :] for g in (0, SUB - 1, SUB)]
            yD[total // 2, :, tile_of(side)] = jnp.where(sub < 4, beyond, last)
            yU[total // 2, :, tile_of(side)] = jnp.where(sub < 4, first, beyond)


def sweep(flags, prev, source, coefs, xL, xR, yA, yB):
    steps, nr, nc = prev.shape
    block = 4
    big = pl.BlockSpec((block, nr, nc), lambda i: (i, 0, 0))
    ext = GROUPS * SUB
    consts = (coefs, xL, xR, yA, yB)
    rest = [(2, ext, LANES), (steps // 2 + 2, SUB, nc), (steps // 2 + 2, SUB, nc)]
    return pl.pallas_call(
        sweep_kernel,
        grid=(steps // block,),
        in_specs=[pl.BlockSpec(memory_space=pltpu.SMEM), big, big] + [whole(a.shape) for a in consts],
        out_specs=[pl.BlockSpec((block, 2, ext, LANES), lambda i: (i, 0, 0, 0))] + [whole(s) for s in rest],
        out_shape=[jax.ShapeDtypeStruct(s, jnp.float32) for s in [(steps, 2, ext, LANES)] + rest],
        scratch_shapes=[
            pltpu.VMEM((2, 2, 2, ext, LANES), jnp.float32),
            pltpu.VMEM((5, 2, ext, LANES), jnp.float32),
            pltpu.VMEM((2, 3, ext, LANES), jnp.float32),
            pltpu.VMEM((8, 3, STRIDE, SUB, LANES), jnp.float32),
            pltpu.VMEM((3, STRIDE, SUB, LANES), jnp.float32),
        ],
        compiler_params=pltpu.CompilerParams(vmem_limit_bytes=16 * MIB),
        name="sweep",
    )(flags, prev, source, *consts)


def split3(x):
    hi = x.astype(jnp.bfloat16)
    left = x - hi.astype(jnp.float32)
    mid = left.astype(jnp.bfloat16)
    low = (left - mid.astype(jnp.float32)).astype(jnp.bfloat16)
    return hi, mid, low


def settle_kernel(
    flags, local, source, coefs, xL, xR, yA, yB, rims, rL, rR, kA, kB, ids, settled, coarse, pack, ring, edge, before, resid
):
    step0 = pl.program_id(0)
    steps = local.shape[0]
    total = steps * pl.num_programs(0)
    lanes, sub = lane_ids(), sub_ids()
    has_left, has_right, has_up, has_down = [(flags[k] != 0) for k in range(4)]
    as_one = lambda mask: jnp.where(mask, 1.0, 0.0)
    only = lambda mask, x: jnp.where(mask, x, 0.0)

    def column(ref, g, lane):
        return jnp.broadcast_to(ref[2, rows_of(g), lane : lane + 1], (SUB, LANES))

    def halo_plane(p, k):
        slab = total + p // 2
        return halo_rows(
            present(yB[slab, :, tile_of(k)], flags[3]), present(yA[slab, :, tile_of(k)], flags[2]), p % 2, sub
        )

    @pl.when(step0 == 0)
    def _():
        across = lambda k: as_one((lanes < 2) & has_left) if k == 0 else as_one((lanes > LANES - 3) & has_right)
        for g in range(GROUPS):
            if g < SUB:
                down = only(sub < 2, as_one(has_up)) if g == 0 else only(sub > 5, as_one(has_down)) if g == SUB - 1 else 0.0 * as_one(sub < 0)
            else:
                down = as_one(sub >= 0)
            for k in range(2):
                copies = (1.0 + across(k)) * (1.0 + down) - 1.0
                weight = coefs[WEIGHT, rows_of(g), tile_of(k)] if g < SUB else halo_plane(WEIGHT, k)
                ring[0, k, g] = weight / (weight + copies)
                ring[1, k, g] = 1.0 / (weight + copies)
            for side, got, xref, lane, keep, back in ((0, rL, xL, 4 * WEIGHT + 2, 0, LANES - 1), (1, rR, xR, 4 * WEIGHT, 2, 1)):
                arrived = present(got[rows_of(g), :], flags[side])
                fwd_above = present(kA[total // 2 + 1, :, tile_of(side)], flags[side] * flags[2])
                fwd_below = present(kB[total // 2 + 1, :, tile_of(side)], flags[side] * flags[3])
                if g == 0:
                    extra = only(sub < 2, fwd_above)
                elif g == SUB - 1:
                    extra = only(sub > 5, fwd_below)
                elif g == SUB:
                    extra = only(sub == SUB - 1, fwd_above) + only(sub == 0, fwd_below)
                else:
                    extra = jnp.zeros((SUB, LANES), jnp.float32)
                value = arrived + extra
                if g < SUB:
                    mine = rims[side, rows_of(g), :]
                    if g == 0:
                        mine = mine + only((sub < 2) & has_up, kA[total // 2, :, tile_of(side)])
                    if g == SUB - 1:
                        mine = mine + only((sub > 5) & has_down, kB[total // 2, :, tile_of(side)])
                    weight = column(xref, g, lane)
                    copies = 2.0 * (1.0 + down) - 1.0
                    outer = (weight * arrived + (pltpu.roll(mine, back, 1) + extra)) / (weight + copies)
                    value = jnp.where(lax.rem(lanes, 4) == keep, outer, value)
                edge[side, g] = value
        for k in range(2):
            for g in range(SUB):
                own = lambda p: coefs[p, rows_of(g), tile_of(k)]
                neighbour = present(column(xL, g, 4 * EAST + 2), flags[0]) if k == 0 else coefs[EAST, rows_of(g), tile_of(0)]
                west = west_of(jnp.where(lanes == LANES - 1, neighbour, own(EAST)))
                above = halo_plane(SOUTH, k) if g == 0 else coefs[SOUTH, rows_of(g - 1), tile_of(k)]
                north = pltpu.roll(jnp.where(sub == SUB - 1, above, own(SOUTH)), 1, 0)
                pack[0, k, g] = west
                pack[1, k, g] = north
                pack[2, k, g] = own(STORAGE) + own(LEAKAGE) + own(EAST) + west + own(SOUTH) + north
                before[k, g] = own(START)

    def step(i, t, odd):
        slab = t // 2
        mid = []
        for k in range(2):
            from_above, from_below = kA[slab, :, tile_of(k)], kB[slab, :, tile_of(k)]
            if odd:
                from_above, from_below = half_turn(from_above), half_turn(from_below)
            values = []
            for g in range(GROUPS):
                side = rolled(edge[k, g], -4 * t - 1 if k == 0 else LANES - 2 - 4 * t)
                extra = only(lanes < 2 if k == 0 else lanes > LANES - 3, side)
                here = local[i, k, rows_of(g), :]
                if g == 0:
                    extra = extra + only((sub < 2) & has_up, from_above)
                elif g == SUB - 1:
                    extra = extra + only((sub > 5) & has_down, from_below)
                elif g == SUB:
                    extra = extra + here
                    here = jnp.where(sub < 4, from_below, from_above)
                values.append((ring[0, k, g] * here + ring[1, k, g] * extra, side))
            mid.append(values)
        for k in range(2):
            for g in range(SUB):
                x = mid[k][g][0]
                if k == 0:
                    west = jnp.where(lanes == LANES - 1, mid[0][g][1], x)
                    east = jnp.where(lanes == 0, mid[1][g][0], x)
                else:
                    west = jnp.where(lanes == LANES - 1, mid[0][g][0], x)
                    east = jnp.where(lanes == 0, mid[1][g][1], x)
                north = jnp.where(sub == SUB - 1, mid[k][(g + GROUPS - 1) % GROUPS][0], x)
                south = jnp.where(sub == 0, mid[k][g + 1][0], x)
                around = (coefs[EAST, rows_of(g), tile_of(k)] * east_of(east) + pack[0, k, g] * west_of(west)) + (
                    coefs[SOUTH, rows_of(g), tile_of(k)] * pltpu.roll(south, SUB - 1, 0) + pack[1, k, g] * pltpu.roll(north, 1, 0)
                )
                value = (source[i, rows_of(g), tile_of(k)] + coefs[STORAGE, rows_of(g), tile_of(k)] * before[k, g]) - (
                    pack[2, k, g] * x - around
                )
                resid[k, pl.ds(t * 64 + g * SUB, SUB), :] = value
                before[k, g] = x
                settled[i, rows_of(g), tile_of(k)] = x

    def pair(q, _):
        for odd in range(2):
            step(2 * q + odd, step0 * steps + 2 * q + odd, odd)
        return 0

    lax.fori_loop(0, steps // 2, pair, 0)

    @pl.when(step0 == pl.num_programs(0) - 1)
    def _():
        aggs = lax.broadcasted_iota(jnp.int32, (64, 2 * LANES), 0)

        def one_row(r, acc):
            picked = jnp.broadcast_to(ids[pl.ds(r, 1), :] - flags[4], (64, 2 * LANES))
            hot = jnp.where(picked == aggs, 1.0, 0.0).astype(jnp.bfloat16)
            values = jnp.concatenate([resid[k, pl.ds(r, total, stride=64), :] for k in range(2)], axis=1)
            parts = jnp.concatenate(split3(values), axis=0)
            return acc + lax.dot_general(parts, hot, (((1,), (1,)), ((), ())), preferred_element_type=jnp.float32)

        def rows4(r, acc):
            for o in range(4):
                acc = one_row(4 * r + o, acc)
            return acc

        acc = lax.fori_loop(0, 16, rows4, jnp.zeros((3 * total, 64), jnp.float32))
        sums = acc[:total] + acc[total : 2 * total] + acc[2 * total :]
        block = jnp.concatenate([sums[: total // 2], sums[total // 2 :]], axis=1)
        coarse[0] = block


def settle(flags, local, source, coefs, xL, xR, yA, yB, rims, rL, rR, kA, kB, ids):
    steps, nr, nc = source.shape
    block = 4
    ext = GROUPS * SUB
    big = pl.BlockSpec((block, nr, nc), lambda i: (i, 0, 0))
    consts = (coefs, xL, xR, yA, yB, rims, rL, rR, kA, kB, ids)
    shapes = [(steps, nr, nc), (1, steps // 2, LANES)]
    return pl.pallas_call(
        settle_kernel,
        grid=(steps // block,),
        in_specs=[
            pl.BlockSpec(memory_space=pltpu.SMEM),
            pl.BlockSpec((block, 2, ext, LANES), lambda i: (i, 0, 0, 0)),
            big,
        ]
        + [whole(a.shape) for a in consts],
        out_specs=[big, whole(shapes[1])],
        out_shape=[jax.ShapeDtypeStruct(s, jnp.float32) for s in shapes],
        scratch_shapes=[
            pltpu.VMEM((3, 2, SUB, SUB, LANES), jnp.float32),
            pltpu.VMEM((2, 2, GROUPS, SUB, LANES), jnp.float32),
            pltpu.VMEM((2, GROUPS, SUB, LANES), jnp.float32),
            pltpu.VMEM((2, SUB, SUB, LANES), jnp.float32),
            pltpu.VMEM((2, steps * nr, LANES), jnp.float32),
        ],
        compiler_params=pltpu.CompilerParams(vmem_limit_bytes=20 * MIB),
        name="settle",
    )(flags, local, source, *consts)


def finish_kernel(flags, every, inverse, settled, ids, out, table, stacked):
    step0 = pl.program_id(0)
    steps = settled.shape[0]
    half = every.shape[1]
    lanes = lane_ids()

    @pl.when(step0 == 0)
    def _():
        for d in range(every.shape[0] // 2):
            for g in range(half // SUB):
                a, b = [every[2 * d + o, rows_of(g), :] for o in range(2)]
                stacked[rows_of(g), tile_of(d)] = jnp.where(lanes < LANES // 2, a, pltpu.roll(b, LANES // 2, 1))
                stacked[half + g * SUB : half + (g + 1) * SUB, tile_of(d)] = jnp.where(
                    lanes < LANES // 2, pltpu.roll(a, LANES // 2, 1), b
                )
        product = lax.dot_general(
            stacked[...],
            inverse[...],
            (((1,), (1,)), ((), ())),
            precision=lax.Precision.HIGHEST,
            preferred_element_type=jnp.float32,
        )
        table[...] = jnp.concatenate([product, product], axis=1)

    def step(i, _):
        t = step0 * steps + i
        row = jnp.broadcast_to(table[pl.ds(t, 1), :], (SUB, LANES))
        for g in range(SUB):
            for k in range(2):
                picked = ids[rows_of(g), tile_of(k)] - flags[4]
                out[i, rows_of(g), tile_of(k)] = settled[i, rows_of(g), tile_of(k)] + jnp.take_along_axis(row, picked, axis=1)
        return 0

    lax.fori_loop(0, steps, step, 0)


def finish(flags, every, inverse, settled, ids):
    steps, nr, nc = settled.shape
    block = 8
    big = pl.BlockSpec((block, nr, nc), lambda i: (i, 0, 0))
    return pl.pallas_call(
        finish_kernel,
        grid=(steps // block,),
        in_specs=[pl.BlockSpec(memory_space=pltpu.SMEM), whole(every.shape), whole(inverse.shape), big, whole(ids.shape)],
        out_specs=big,
        out_shape=jax.ShapeDtypeStruct(settled.shape, jnp.float32),
        scratch_shapes=[pltpu.VMEM((steps, LANES), jnp.float32), pltpu.VMEM((steps, inverse.shape[1]), jnp.float32)],
        compiler_params=pltpu.CompilerParams(vmem_limit_bytes=20 * MIB),
        name="finish",
    )(flags, every, inverse, settled, ids)


def neighbours(low, high, axis):
    count = lax.axis_size(axis)
    forward = [(i, (i + 1) % count) for i in range(count)]
    backward = [(target, source) for source, target in forward]
    return lax.ppermute(high, axis, forward), lax.ppermute(low, axis, backward)


def gather_all(block):
    count = lax.axis_size("gx") * lax.axis_size("gy")
    block = block.reshape(1, 1, -1)
    every = lax.all_to_all(jnp.broadcast_to(block, (count,) + block.shape[1:]), ("gx", "gy"), 0, 0)
    return every.reshape(count, -1, LANES)


def shards(
    prev_wave,
    source,
    start_state,
    storage,
    leakage,
    cond_east,
    cond_south,
    owner_weight,
    aggregate,
    coarse_inverse,
):
    gx, gy = lax.axis_index("gx"), lax.axis_index("gy")
    nx, ny = lax.axis_size("gx"), lax.axis_size("gy")
    flags = jnp.stack([gx, nx - 1 - gx, gy, ny - 1 - gy, (gx * ny + gy) * coarse_inverse.shape[0]]).astype(jnp.int32)
    planes = (start_state, storage, leakage, cond_east, cond_south, owner_weight)
    coefs, to_left, to_right, to_up, to_down = pack(flags, prev_wave, source, planes)
    xL, xR = neighbours(to_left, to_right, "gx")
    wide = lambda first, second: jnp.concatenate([first, second], -1)
    slab = to_up.shape[0] - 3
    to_up = to_up.at[slab:].set(wide(xL[:, :SUB], xR[:, :SUB]))
    to_down = to_down.at[slab:].set(wide(xL[:, -SUB:], xR[:, -SUB:]))
    yA, yB = neighbours(to_up, to_down, "gy")
    local, rims, yU, yD = sweep(flags, prev_wave, source, coefs, xL, xR, yA, yB)
    rL, rR = neighbours(rims[0], rims[1], "gx")
    half = SUB // 2
    around = wide(rL, rR)
    yU = yU.at[-1].set(jnp.concatenate([around[:half], around[-half:]], 0))
    yD = yD.at[-1].set(jnp.concatenate([around[-SUB : -half], around[-SUB - half : -SUB]], 0))
    kA, kB = neighbours(yU, yD, "gy")
    settled, coarse = settle(flags, local, source, coefs, xL, xR, yA, yB, rims, rL, rR, kA, kB, aggregate)
    every = gather_all(coarse)
    return finish(flags, every, coarse_inverse, settled, aggregate)


def solution(mesh):
    return jax.shard_map(
        shards,
        mesh=mesh,
        in_specs=(
            P(None, "gy", "gx"),
            P(None, "gy", "gx"),
            P("gy", "gx"),
            P("gy", "gx"),
            P("gy", "gx"),
            P("gy", "gx"),
            P("gy", "gx"),
            P("gy", "gx"),
            P("gy", "gx"),
            P(("gx", "gy"), None),
        ),
        out_specs=P(None, "gy", "gx"),
        check_vma=False,
    )
```

```python
import functools
import math

import jax
import jax.numpy as jnp
import numpy as np
from jax import lax
from jax.experimental import pallas as pl
from jax.experimental.pallas import tpu as pltpu
from jax.sharding import PartitionSpec as P

DEG = 8
OV = 2
STRIDE = 9
LANES = 128
SUB = 8


cheb_theta = 1.0
cheb_delta = 0.95


def horner_coefficients():
    t8 = np.array([1.0, -32.0, 160.0, -256.0, 128.0])
    u_scale = 1.0 / cheb_delta**2
    at_one = sum(c * u_scale**k for k, c in enumerate(t8))
    g = -np.array([c * u_scale**k for k, c in enumerate(t8)]) / at_one
    g[0] += 1.0
    q = np.zeros(4)
    total = 0.0
    for k in range(4):
        total += g[k]
        q[k] = total
    return q


Q_COEF = horner_coefficients()


def sub_ids():
    return lax.broadcasted_iota(jnp.int32, (SUB, LANES), 0)


def lane_ids():
    return lax.broadcasted_iota(jnp.int32, (SUB, LANES), 1)


def row_ids_of(j):
    return lax.broadcasted_iota(jnp.int32, (SUB, LANES), 0) * STRIDE + j


def east_of(x):
    return pltpu.roll(x, LANES - 1, 1)


def west_of(x):
    return pltpu.roll(x, 1, 1)


def south_list(xs):
    return xs[1:] + [pltpu.roll(xs[0], SUB - 1, 0)]


def north_list(xs):
    return [pltpu.roll(xs[-1], 1, 0)] + xs[:-1]


def off_diagonal(xs, east, south):
    from_north = north_list([s * x for s, x in zip(south, xs)])
    from_south = [s * x for s, x in zip(south, south_list(xs))]
    out = []
    for j, x in enumerate(xs):
        out.append((west_of(east[j] * x) + east[j] * east_of(x)) + (from_north[j] + from_south[j]))
    return out


GROUPS = 9
PLANES = 6
MIB = 1024 * 1024
START, STORAGE, LEAKAGE, EAST, SOUTH, WEIGHT = range(PLANES)


def tile_of(k):
    return slice(k * LANES, (k + 1) * LANES)


def rows_of(g):
    return slice(g * SUB, (g + 1) * SUB)


def rows(j):
    return pl.ds(j, SUB, stride=STRIDE)


def rolled(x, amount):
    return pltpu.roll(x, lax.rem(amount + 4 * LANES, LANES), 1)


def half_turn(x):
    return pltpu.roll(x, SUB // 2, 0)


def whole(shape):
    return pl.BlockSpec(shape, lambda i: (0,) * len(shape))


def edge_rows_kernel(
    flags, prev, source, start, storage, leakage, east, south, weight, coef, to_up, to_down, waves, planes, numbers, sems
):
    total = prev.shape[0]
    lanes, sub = lane_ids(), sub_ids()
    copies = []

    def fetch(source_ref, target_ref):
        copies.append(pltpu.make_async_copy(source_ref, target_ref, sems.at[len(copies)]))
        copies[-1].start()

    for end, g in ((0, 0), (1, SUB - 1)):
        for array, ref in ((0, prev), (1, source)):
            fetch(ref.at[:, rows_of(g), :], waves.at[array, end])
    for p, ref in enumerate((start, storage, leakage, east, south)):
        fetch(ref, planes.at[p])
    fetch(weight, numbers)
    for copy in copies:
        copy.wait()

    def slabs(slab, even, odd):
        for k in range(2):
            to_up[slab, :, tile_of(k)] = jnp.where(sub < 4, even(0, k), half_turn(odd(0, k)))
            to_down[slab, :, tile_of(k)] = jnp.where(sub < 4, half_turn(odd(1, k)), even(1, k))

    for p in range(PLANES):
        for g in range(SUB):
            for k in range(2):
                ref = numbers if p == WEIGHT else planes.at[p]
                value = ref[rows_of(g), tile_of(k)].astype(jnp.float32)
                if p == EAST and k == 1:
                    value = jnp.where((lanes == LANES - 1) & (flags[1] == 0), 0.0, value)
                if p == SOUTH and g == SUB - 1:
                    value = jnp.where((sub == SUB - 1) & (flags[3] == 0), 0.0, value)
                coef[p, rows_of(g), tile_of(k)] = value

    plane = lambda p: lambda end, k: coef[p, rows_of(end * (SUB - 1)), tile_of(k)]
    for q in range(PLANES // 2):
        slabs(total + q, plane(2 * q), plane(2 * q + 1))

    def pair(q, _):
        for array in range(2):
            wave = lambda i: lambda end, k: waves[array, end, i, :, tile_of(k)]
            slabs(array * (total // 2) + q, wave(2 * q), wave(2 * q + 1))
        return 0

    lax.fori_loop(0, total // 2, pair, 0)


def edge_rows(flags, prev, source, planes):
    steps, nr, nc = prev.shape
    out = jax.ShapeDtypeStruct((steps + PLANES // 2, SUB, nc), jnp.float32)
    vmem = pl.BlockSpec(memory_space=pltpu.VMEM)
    return pl.pallas_call(
        edge_rows_kernel,
        in_specs=[pl.BlockSpec(memory_space=pltpu.SMEM)] + [pl.BlockSpec(memory_space=pltpu.HBM)] * (2 + PLANES),
        out_specs=[vmem, vmem, vmem],
        out_shape=[jax.ShapeDtypeStruct((PLANES, nr, nc), jnp.float32), out, out],
        scratch_shapes=[
            pltpu.VMEM((2, 2, steps, SUB, nc), jnp.float32),
            pltpu.VMEM((PLANES - 1, nr, nc), jnp.float32),
            pltpu.VMEM((nr, nc), jnp.int32),
            pltpu.SemaphoreType.DMA((PLANES + 4,)),
        ],
        compiler_params=pltpu.CompilerParams(vmem_limit_bytes=60 * MIB),
        name="rows",
    )(flags, prev, source, *planes)


def put_sides(left, right, array, slot, g, value_left, value_right):
    lanes = lane_ids()
    here = (lanes >= slot) & (lanes < slot + 3)
    left[array, rows_of(g), :] = jnp.where(here, rolled(value_left, slot), left[array, rows_of(g), :])
    right[array, rows_of(g), :] = jnp.where(here, rolled(value_right, slot + 3), right[array, rows_of(g), :])


def pack_kernel(prev, source, coef, to_left, to_right):
    step0 = pl.program_id(0)
    steps = prev.shape[0]

    @pl.when(step0 == 0)
    def _():
        for array in range(3):
            to_left[array] = jnp.zeros_like(to_left[array])
            to_right[array] = jnp.zeros_like(to_right[array])
        for p in range(PLANES):
            for g in range(SUB):
                put_sides(to_left, to_right, 2, 4 * p, g, *[coef[p, rows_of(g), tile_of(k)] for k in range(2)])

    def step(i, _):
        for array, ref in ((0, prev), (1, source)):
            for g in range(SUB):
                values = [ref[i, rows_of(g), tile_of(k)] for k in range(2)]
                put_sides(to_left, to_right, array, 4 * (step0 * steps + i), g, *values)
        return 0

    lax.fori_loop(0, steps, step, 0)


def pack(prev, source, coefs):
    steps, nr, nc = prev.shape
    block = 8
    big = pl.BlockSpec((block, nr, nc), lambda i: (i, 0, 0))
    shape = (3, nr, LANES)
    return pl.pallas_call(
        pack_kernel,
        grid=(steps // block,),
        in_specs=[big, big, whole(coefs.shape)],
        out_specs=[whole(shape)] * 2,
        out_shape=[jax.ShapeDtypeStruct(shape, jnp.float32)] * 2,
        compiler_params=pltpu.CompilerParams(vmem_limit_bytes=16 * MIB),
        cost_estimate=pl.CostEstimate(flops=20_000_000, bytes_accessed=16_000_000, transcendentals=0),
        name="pack",
    )(prev, source, coefs)


def corners_kernel(flags, left, right, yA, yB, to_left, to_right):
    total = yA.shape[0] - PLANES // 2
    sub = sub_ids()
    for array in range(3):
        for ref, out in ((left, to_left), (right, to_right)):
            out[array, : SUB * SUB, :] = ref[array]
            out[array, rows_of(SUB), :] = jnp.zeros((SUB, LANES), jnp.float32)

    def both(slab, array, slot):
        for odd in range(2):
            values = [halo_rows(yB[slab, :, tile_of(k)], yA[slab, :, tile_of(k)], odd, sub) for k in range(2)]
            put_sides(to_left, to_right, array, slot + 4 * odd, SUB, *values)

    for q in range(PLANES // 2):
        for odd in range(2):
            values = [
                halo_rows(
                    present(yB[total + q, :, tile_of(k)], flags[3]), present(yA[total + q, :, tile_of(k)], flags[2]), odd, sub
                )
                for k in range(2)
            ]
            put_sides(to_left, to_right, 2, 4 * (2 * q + odd), SUB, *values)

    def pair(q, _):
        for array in range(2):
            both(array * (total // 2) + q, array, 8 * q)
        return 0

    lax.fori_loop(0, total // 2, pair, 0)


def corners(flags, left, right, yA, yB):
    vmem = pl.BlockSpec(memory_space=pltpu.VMEM)
    out = jax.ShapeDtypeStruct((3, GROUPS * SUB, LANES), jnp.float32)
    return pl.pallas_call(
        corners_kernel,
        in_specs=[pl.BlockSpec(memory_space=pltpu.SMEM)] + [vmem] * 4,
        out_specs=[vmem, vmem],
        out_shape=[out, out],
        compiler_params=pltpu.CompilerParams(vmem_limit_bytes=8 * MIB),
        name="corners",
    )(flags, left, right, yA, yB)


def windows_of(left, right, halo_left, halo_right, lanes):
    return (
        jnp.where(lanes < LANES - 3, left, halo_left),
        jnp.where(lanes < LANES // 2, right, left),
        jnp.where(lanes < 3, halo_right, right),
    )


def halo_rows(below, above, odd, sub):
    if odd:
        return half_turn(jnp.where(sub < 4, above, below))
    return jnp.where(sub < 4, below, above)


def present(x, flag):
    return jnp.where(flag != 0, x, 0.0)


def sweep_kernel(flags, prev, source, coefs, xL, xR, yA, yB, out, rims, yU, yD, tiles, ctiles, halo, coef, carry):
    step0 = pl.program_id(0)
    steps = prev.shape[0]
    total = steps * pl.num_programs(0)
    lanes, sub = lane_ids(), sub_ids()

    def window_set(j, left, right, array, slot):
        return windows_of(
            left, right, rolled(halo[0, array, rows(j), :], LANES - 3 - slot), rolled(halo[1, array, rows(j), :], -slot), lanes
        )

    breaks = (LANES - 4, LANES // 2 - 1, 2)
    outer = (LANES - 3, -1, 2)

    @pl.when(step0 == 0)
    def _():
        for array in range(3):
            for side, ref in ((0, xL), (1, xR)):
                for g in range(GROUPS):
                    value = ref[array, rows_of(g), :]
                    halo[side, array, rows_of(g), :] = present(value, flags[side]) if array == 2 else value
        for p in range(5):
            slab = total + p // 2
            for k in range(2):
                for g in range(SUB):
                    ctiles[p, k, rows_of(g), :] = coefs[p, rows_of(g), tile_of(k)]
                ctiles[p, k, rows_of(SUB), :] = halo_rows(
                    present(yB[slab, :, tile_of(k)], flags[3]), present(yA[slab, :, tile_of(k)], flags[2]), p % 2, sub
                )
        planes = [
            [window_set(j, ctiles[p, 0, rows(j), :], ctiles[p, 1, rows(j), :], 2, 4 * p) for j in range(STRIDE)]
            for p in range(5)
        ]
        for w in range(3):
            start, storage, leakage, east, south = [[planes[p][j][w] for j in range(STRIDE)] for p in range(5)]
            east = [jnp.where(lanes == breaks[w], 0.0, e) for e in east]
            north = north_list(south)
            diag, scale = [], []
            for j in range(STRIDE):
                d = storage[j] + leakage[j] + east[j] + west_of(east[j]) + south[j] + north[j]
                row = row_ids_of(j)
                inner = ((row < 66) | (row > 69)) & (lanes != outer[w]) & (d > 0.0)
                diag.append(d)
                scale.append(jnp.where(inner, 1.0 / jnp.sqrt(jnp.where(inner, d, 1.0)), 0.0))
            scale_south = south_list(scale)
            for j in range(STRIDE):
                carry[w, j] = start[j]
                coef[0, w, j] = east[j] * scale[j] * east_of(scale[j])
                coef[1, w, j] = south[j] * scale[j] * scale_south[j]
                coef[2, w, j] = storage[j]
                coef[3, w, j] = diag[j]
                coef[4, w, j] = east[j]
                coef[5, w, j] = south[j]
                coef[6, w, j] = scale[j]
                coef[7, w, j] = scale[j] * np.float32(Q_COEF[3])
        for side in range(2):
            rims[side] = jnp.zeros_like(rims[side])

    def step(i, t, odd):
        for array, ref in ((0, prev), (1, source)):
            slab = array * (total // 2) + t // 2
            for k in range(2):
                for g in range(SUB):
                    tiles[odd, array, k, rows_of(g), :] = ref[i, rows_of(g), tile_of(k)]
                tiles[odd, array, k, rows_of(SUB), :] = halo_rows(yB[slab, :, tile_of(k)], yA[slab, :, tile_of(k)], odd, sub)
        x0s, srcs = [
            [window_set(j, tiles[odd, a, 0, rows(j), :], tiles[odd, a, 1, rows(j), :], a, 4 * t) for j in range(STRIDE)]
            for a in range(2)
        ]
        every = range(3)
        x0 = [[x0s[j][w] for j in range(STRIDE)] for w in every]
        table = lambda n, w: [coef[n, w, j] for j in range(STRIDE)]
        full = [off_diagonal(x0[w], table(4, w), table(5, w)) for w in every]
        z = [
            [
                coef[6, w, j] * ((srcs[j][w] + coef[2, w, j] * carry[w, j]) + (full[w][j] - coef[3, w, j] * x0[w][j]))
                for j in range(STRIDE)
            ]
            for w in every
        ]
        apply = lambda v: [off_diagonal(v[w], table(0, w), table(1, w)) for w in every]
        base = [[a + b for a, b in zip(p, q)] for p, q in zip(z, apply(z))]
        y = base
        for k in (2, 1, 0):
            y = apply(apply(y))
            ratio = np.float32(Q_COEF[k] / Q_COEF[3])
            y = [[a + ratio * b for a, b in zip(p, q)] for p, q in zip(y, base)]
        result = [[x0[w][j] + coef[7, w, j] * y[w][j] for j in range(STRIDE)] for w in every]
        slot = 4 * t
        here = (lanes >= slot) & (lanes < slot + 3)
        for j in range(STRIDE):
            a, b, c = result[0][j], result[1][j], result[2][j]
            left = jnp.where(lanes < 96, a, b)
            right = jnp.where(lanes < 32, b, c)
            out[i, 0, rows(j), :] = left
            out[i, 1, rows(j), :] = right
            fresh = windows_of(left, right, a, c, lanes)
            for w in range(3):
                carry[w, j] = fresh[w]
            rims[0, rows(j), :] = jnp.where(here, rolled(a, slot + 2), rims[0, rows(j), :])
            rims[1, rows(j), :] = jnp.where(here, rolled(c, slot + 1), rims[1, rows(j), :])

    def pair(q, _):
        for odd in range(2):
            step(2 * q + odd, step0 * steps + 2 * q + odd, odd)
        kept = (sub < 2) | (sub > 5)
        slab = step0 * (steps // 2) + q
        for k in range(2):
            down, up = [], []
            for odd in range(2):
                first, last, beyond = [out[2 * q + odd, k, rows_of(g), :] for g in (0, SUB - 1, SUB)]
                down.append(jnp.where(sub < 4, beyond, last))
                up.append(jnp.where(sub < 4, first, beyond))
            yD[slab, :, tile_of(k)] = jnp.where(kept, down[0], half_turn(down[1]))
            yU[slab, :, tile_of(k)] = jnp.where(kept, up[0], half_turn(up[1]))
        return 0

    lax.fori_loop(0, steps // 2, pair, 0)

    @pl.when(step0 == pl.num_programs(0) - 1)
    def _():
        for side in range(2):
            first, last, beyond = [rims[side, rows_of(g), :] for g in (0, SUB - 1, SUB)]
            yD[total // 2, :, tile_of(side)] = jnp.where(sub < 4, beyond, last)
            yU[total // 2, :, tile_of(side)] = jnp.where(sub < 4, first, beyond)


def sweep(flags, prev, source, coefs, xL, xR, yA, yB):
    steps, nr, nc = prev.shape
    block = 4
    big = pl.BlockSpec((block, nr, nc), lambda i: (i, 0, 0))
    ext = GROUPS * SUB
    consts = (coefs, xL, xR, yA, yB)
    rest = [(2, ext, LANES), (steps // 2 + 2, SUB, nc), (steps // 2 + 2, SUB, nc)]
    return pl.pallas_call(
        sweep_kernel,
        grid=(steps // block,),
        in_specs=[pl.BlockSpec(memory_space=pltpu.SMEM), big, big] + [whole(a.shape) for a in consts],
        out_specs=[pl.BlockSpec((block, 2, ext, LANES), lambda i: (i, 0, 0, 0))] + [whole(s) for s in rest],
        out_shape=[jax.ShapeDtypeStruct(s, jnp.float32) for s in [(steps, 2, ext, LANES)] + rest],
        scratch_shapes=[
            pltpu.VMEM((2, 2, 2, ext, LANES), jnp.float32),
            pltpu.VMEM((5, 2, ext, LANES), jnp.float32),
            pltpu.VMEM((2, 3, ext, LANES), jnp.float32),
            pltpu.VMEM((8, 3, STRIDE, SUB, LANES), jnp.float32),
            pltpu.VMEM((3, STRIDE, SUB, LANES), jnp.float32),
        ],
        compiler_params=pltpu.CompilerParams(vmem_limit_bytes=16 * MIB),
        name="sweep",
    )(flags, prev, source, *consts)


def split3(x):
    hi = x.astype(jnp.bfloat16)
    left = x - hi.astype(jnp.float32)
    mid = left.astype(jnp.bfloat16)
    low = (left - mid.astype(jnp.float32)).astype(jnp.bfloat16)
    return hi, mid, low


def settle_kernel(
    flags, local, source, coefs, xL, xR, yA, yB, rims, rL, rR, kA, kB, ids, settled, coarse, pack, ring, edge, before, resid
):
    step0 = pl.program_id(0)
    steps = local.shape[0]
    total = steps * pl.num_programs(0)
    lanes, sub = lane_ids(), sub_ids()
    has_left, has_right, has_up, has_down = [(flags[k] != 0) for k in range(4)]
    as_one = lambda mask: jnp.where(mask, 1.0, 0.0)
    only = lambda mask, x: jnp.where(mask, x, 0.0)

    def column(ref, g, lane):
        return jnp.broadcast_to(ref[2, rows_of(g), lane : lane + 1], (SUB, LANES))

    def halo_plane(p, k):
        slab = total + p // 2
        return halo_rows(
            present(yB[slab, :, tile_of(k)], flags[3]), present(yA[slab, :, tile_of(k)], flags[2]), p % 2, sub
        )

    @pl.when(step0 == 0)
    def _():
        across = lambda k: as_one((lanes < 2) & has_left) if k == 0 else as_one((lanes > LANES - 3) & has_right)
        for g in range(GROUPS):
            if g < SUB:
                down = only(sub < 2, as_one(has_up)) if g == 0 else only(sub > 5, as_one(has_down)) if g == SUB - 1 else 0.0 * as_one(sub < 0)
            else:
                down = as_one(sub >= 0)
            for k in range(2):
                copies = (1.0 + across(k)) * (1.0 + down) - 1.0
                weight = coefs[WEIGHT, rows_of(g), tile_of(k)] if g < SUB else halo_plane(WEIGHT, k)
                ring[0, k, g] = weight / (weight + copies)
                ring[1, k, g] = 1.0 / (weight + copies)
            for side, got, xref, lane, keep, back in ((0, rL, xL, 4 * WEIGHT + 2, 0, LANES - 1), (1, rR, xR, 4 * WEIGHT, 2, 1)):
                arrived = present(got[rows_of(g), :], flags[side])
                fwd_above = present(kA[total // 2 + 1, :, tile_of(side)], flags[side] * flags[2])
                fwd_below = present(kB[total // 2 + 1, :, tile_of(side)], flags[side] * flags[3])
                if g == 0:
                    extra = only(sub < 2, fwd_above)
                elif g == SUB - 1:
                    extra = only(sub > 5, fwd_below)
                elif g == SUB:
                    extra = only(sub == SUB - 1, fwd_above) + only(sub == 0, fwd_below)
                else:
                    extra = jnp.zeros((SUB, LANES), jnp.float32)
                value = arrived + extra
                if g < SUB:
                    mine = rims[side, rows_of(g), :]
                    if g == 0:
                        mine = mine + only((sub < 2) & has_up, kA[total // 2, :, tile_of(side)])
                    if g == SUB - 1:
                        mine = mine + only((sub > 5) & has_down, kB[total // 2, :, tile_of(side)])
                    weight = column(xref, g, lane)
                    copies = 2.0 * (1.0 + down) - 1.0
                    outer = (weight * arrived + (pltpu.roll(mine, back, 1) + extra)) / (weight + copies)
                    value = jnp.where(lax.rem(lanes, 4) == keep, outer, value)
                edge[side, g] = value
        for k in range(2):
            for g in range(SUB):
                own = lambda p: coefs[p, rows_of(g), tile_of(k)]
                neighbour = present(column(xL, g, 4 * EAST + 2), flags[0]) if k == 0 else coefs[EAST, rows_of(g), tile_of(0)]
                west = west_of(jnp.where(lanes == LANES - 1, neighbour, own(EAST)))
                above = halo_plane(SOUTH, k) if g == 0 else coefs[SOUTH, rows_of(g - 1), tile_of(k)]
                north = pltpu.roll(jnp.where(sub == SUB - 1, above, own(SOUTH)), 1, 0)
                pack[0, k, g] = west
                pack[1, k, g] = north
                pack[2, k, g] = own(STORAGE) + own(LEAKAGE) + own(EAST) + west + own(SOUTH) + north
                before[k, g] = own(START)

    def step(i, t, odd):
        slab = t // 2
        mid = []
        for k in range(2):
            from_above, from_below = kA[slab, :, tile_of(k)], kB[slab, :, tile_of(k)]
            if odd:
                from_above, from_below = half_turn(from_above), half_turn(from_below)
            values = []
            for g in range(GROUPS):
                side = rolled(edge[k, g], -4 * t - 1 if k == 0 else LANES - 2 - 4 * t)
                extra = only(lanes < 2 if k == 0 else lanes > LANES - 3, side)
                here = local[i, k, rows_of(g), :]
                if g == 0:
                    extra = extra + only((sub < 2) & has_up, from_above)
                elif g == SUB - 1:
                    extra = extra + only((sub > 5) & has_down, from_below)
                elif g == SUB:
                    extra = extra + here
                    here = jnp.where(sub < 4, from_below, from_above)
                values.append((ring[0, k, g] * here + ring[1, k, g] * extra, side))
            mid.append(values)
        for k in range(2):
            for g in range(SUB):
                x = mid[k][g][0]
                if k == 0:
                    west = jnp.where(lanes == LANES - 1, mid[0][g][1], x)
                    east = jnp.where(lanes == 0, mid[1][g][0], x)
                else:
                    west = jnp.where(lanes == LANES - 1, mid[0][g][0], x)
                    east = jnp.where(lanes == 0, mid[1][g][1], x)
                north = jnp.where(sub == SUB - 1, mid[k][(g + GROUPS - 1) % GROUPS][0], x)
                south = jnp.where(sub == 0, mid[k][g + 1][0], x)
                around = (coefs[EAST, rows_of(g), tile_of(k)] * east_of(east) + pack[0, k, g] * west_of(west)) + (
                    coefs[SOUTH, rows_of(g), tile_of(k)] * pltpu.roll(south, SUB - 1, 0) + pack[1, k, g] * pltpu.roll(north, 1, 0)
                )
                value = (source[i, rows_of(g), tile_of(k)] + coefs[STORAGE, rows_of(g), tile_of(k)] * before[k, g]) - (
                    pack[2, k, g] * x - around
                )
                resid[k, pl.ds(t * 64 + g * SUB, SUB), :] = value
                before[k, g] = x
                settled[i, rows_of(g), tile_of(k)] = x

    def pair(q, _):
        for odd in range(2):
            step(2 * q + odd, step0 * steps + 2 * q + odd, odd)
        return 0

    lax.fori_loop(0, steps // 2, pair, 0)

    @pl.when(step0 == pl.num_programs(0) - 1)
    def _():
        aggs = lax.broadcasted_iota(jnp.int32, (64, 2 * LANES), 0)

        def one_row(r, acc):
            picked = jnp.broadcast_to(ids[pl.ds(r, 1), :] - flags[4], (64, 2 * LANES))
            hot = jnp.where(picked == aggs, 1.0, 0.0).astype(jnp.bfloat16)
            values = jnp.concatenate([resid[k, pl.ds(r, total, stride=64), :] for k in range(2)], axis=1)
            parts = jnp.concatenate(split3(values), axis=0)
            return acc + lax.dot_general(parts, hot, (((1,), (1,)), ((), ())), preferred_element_type=jnp.float32)

        def rows4(r, acc):
            for o in range(4):
                acc = one_row(4 * r + o, acc)
            return acc

        acc = lax.fori_loop(0, 16, rows4, jnp.zeros((3 * total, 64), jnp.float32))
        sums = acc[:total] + acc[total : 2 * total] + acc[2 * total :]
        block = jnp.concatenate([sums[: total // 2], sums[total // 2 :]], axis=1)
        coarse[0] = block


def settle(flags, local, source, coefs, xL, xR, yA, yB, rims, rL, rR, kA, kB, ids):
    steps, nr, nc = source.shape
    block = 4
    ext = GROUPS * SUB
    big = pl.BlockSpec((block, nr, nc), lambda i: (i, 0, 0))
    consts = (coefs, xL, xR, yA, yB, rims, rL, rR, kA, kB, ids)
    shapes = [(steps, nr, nc), (1, steps // 2, LANES)]
    return pl.pallas_call(
        settle_kernel,
        grid=(steps // block,),
        in_specs=[
            pl.BlockSpec(memory_space=pltpu.SMEM),
            pl.BlockSpec((block, 2, ext, LANES), lambda i: (i, 0, 0, 0)),
            big,
        ]
        + [whole(a.shape) for a in consts],
        out_specs=[big, whole(shapes[1])],
        out_shape=[jax.ShapeDtypeStruct(s, jnp.float32) for s in shapes],
        scratch_shapes=[
            pltpu.VMEM((3, 2, SUB, SUB, LANES), jnp.float32),
            pltpu.VMEM((2, 2, GROUPS, SUB, LANES), jnp.float32),
            pltpu.VMEM((2, GROUPS, SUB, LANES), jnp.float32),
            pltpu.VMEM((2, SUB, SUB, LANES), jnp.float32),
            pltpu.VMEM((2, steps * nr, LANES), jnp.float32),
        ],
        compiler_params=pltpu.CompilerParams(vmem_limit_bytes=20 * MIB),
        name="settle",
    )(flags, local, source, *consts)


def finish_kernel(flags, every, inverse, settled, ids, out, table, stacked):
    step0 = pl.program_id(0)
    steps = settled.shape[0]
    half = every.shape[1]
    lanes = lane_ids()

    @pl.when(step0 == 0)
    def _():
        for d in range(every.shape[0] // 2):
            for g in range(half // SUB):
                a, b = [every[2 * d + o, rows_of(g), :] for o in range(2)]
                stacked[rows_of(g), tile_of(d)] = jnp.where(lanes < LANES // 2, a, pltpu.roll(b, LANES // 2, 1))
                stacked[half + g * SUB : half + (g + 1) * SUB, tile_of(d)] = jnp.where(
                    lanes < LANES // 2, pltpu.roll(a, LANES // 2, 1), b
                )
        product = lax.dot_general(
            stacked[...],
            inverse[...],
            (((1,), (1,)), ((), ())),
            precision=lax.Precision.HIGHEST,
            preferred_element_type=jnp.float32,
        )
        table[...] = jnp.concatenate([product, product], axis=1)

    def step(i, _):
        t = step0 * steps + i
        row = jnp.broadcast_to(table[pl.ds(t, 1), :], (SUB, LANES))
        for g in range(SUB):
            for k in range(2):
                picked = ids[rows_of(g), tile_of(k)] - flags[4]
                out[i, rows_of(g), tile_of(k)] = settled[i, rows_of(g), tile_of(k)] + jnp.take_along_axis(row, picked, axis=1)
        return 0

    lax.fori_loop(0, steps, step, 0)


def finish(flags, every, inverse, settled, ids):
    steps, nr, nc = settled.shape
    block = 8
    big = pl.BlockSpec((block, nr, nc), lambda i: (i, 0, 0))
    return pl.pallas_call(
        finish_kernel,
        grid=(steps // block,),
        in_specs=[pl.BlockSpec(memory_space=pltpu.SMEM), whole(every.shape), whole(inverse.shape), big, whole(ids.shape)],
        out_specs=big,
        out_shape=jax.ShapeDtypeStruct(settled.shape, jnp.float32),
        scratch_shapes=[pltpu.VMEM((steps, LANES), jnp.float32), pltpu.VMEM((steps, inverse.shape[1]), jnp.float32)],
        compiler_params=pltpu.CompilerParams(vmem_limit_bytes=20 * MIB),
        name="finish",
    )(flags, every, inverse, settled, ids)


def neighbours(low, high, axis):
    count = lax.axis_size(axis)
    forward = [(i, (i + 1) % count) for i in range(count)]
    backward = [(target, source) for source, target in forward]
    return lax.ppermute(high, axis, forward), lax.ppermute(low, axis, backward)


def gather_all(block):
    count = lax.axis_size("gx") * lax.axis_size("gy")
    block = block.reshape(1, 1, -1)
    every = lax.all_to_all(jnp.broadcast_to(block, (count,) + block.shape[1:]), ("gx", "gy"), 0, 0)
    return every.reshape(count, -1, LANES)


def shards(
    prev_wave,
    source,
    start_state,
    storage,
    leakage,
    cond_east,
    cond_south,
    owner_weight,
    aggregate,
    coarse_inverse,
):
    gx, gy = lax.axis_index("gx"), lax.axis_index("gy")
    nx, ny = lax.axis_size("gx"), lax.axis_size("gy")
    flags = jnp.stack([gx, nx - 1 - gx, gy, ny - 1 - gy, (gx * ny + gy) * coarse_inverse.shape[0]]).astype(jnp.int32)
    planes = (start_state, storage, leakage, cond_east, cond_south, owner_weight)
    coefs, to_up, to_down = edge_rows(flags, prev_wave, source, planes)
    yA, yB = neighbours(to_up, to_down, "gy")
    to_left, to_right = pack(prev_wave, source, coefs)
    to_left, to_right = corners(flags, to_left, to_right, yA, yB)
    xL, xR = neighbours(to_left, to_right, "gx")
    local, rims, yU, yD = sweep(flags, prev_wave, source, coefs, xL, xR, yA, yB)
    rL, rR = neighbours(rims[0], rims[1], "gx")
    half = SUB // 2
    around = jnp.concatenate([rL, rR], -1)
    yU = yU.at[-1].set(jnp.concatenate([around[:half], around[-half:]], 0))
    yD = yD.at[-1].set(jnp.concatenate([around[-SUB : -half], around[-SUB - half : -SUB]], 0))
    kA, kB = neighbours(yU, yD, "gy")
    settled, coarse = settle(flags, local, source, coefs, xL, xR, yA, yB, rims, rL, rR, kA, kB, aggregate)
    every = gather_all(coarse)
    return finish(flags, every, coarse_inverse, settled, aggregate)


def solution(mesh):
    return jax.shard_map(
        shards,
        mesh=mesh,
        in_specs=(
            P(None, "gy", "gx"),
            P(None, "gy", "gx"),
            P("gy", "gx"),
            P("gy", "gx"),
            P("gy", "gx"),
            P("gy", "gx"),
            P("gy", "gx"),
            P("gy", "gx"),
            P("gy", "gx"),
            P(("gx", "gy"), None),
        ),
        out_specs=P(None, "gy", "gx"),
        check_vma=False,
    )
```

```python
import functools
import math

import jax
import jax.numpy as jnp
import numpy as np
from jax import lax
from jax.experimental import pallas as pl
from jax.experimental.pallas import tpu as pltpu
from jax.sharding import PartitionSpec as P

DEG = 8
OV = 2
STRIDE = 9
LANES = 128
SUB = 8


cheb_theta = 1.0
cheb_delta = 0.95


def horner_coefficients():
    t8 = np.array([1.0, -32.0, 160.0, -256.0, 128.0])
    u_scale = 1.0 / cheb_delta**2
    at_one = sum(c * u_scale**k for k, c in enumerate(t8))
    g = -np.array([c * u_scale**k for k, c in enumerate(t8)]) / at_one
    g[0] += 1.0
    q = np.zeros(4)
    total = 0.0
    for k in range(4):
        total += g[k]
        q[k] = total
    return q


Q_COEF = horner_coefficients()


def sub_ids():
    return lax.broadcasted_iota(jnp.int32, (SUB, LANES), 0)


def lane_ids():
    return lax.broadcasted_iota(jnp.int32, (SUB, LANES), 1)


def row_ids_of(j):
    return lax.broadcasted_iota(jnp.int32, (SUB, LANES), 0) * STRIDE + j


def east_of(x):
    return pltpu.roll(x, LANES - 1, 1)


def west_of(x):
    return pltpu.roll(x, 1, 1)


def south_list(xs):
    return xs[1:] + [pltpu.roll(xs[0], SUB - 1, 0)]


def north_list(xs):
    return [pltpu.roll(xs[-1], 1, 0)] + xs[:-1]


def off_diagonal(xs, east, south):
    from_north = north_list([s * x for s, x in zip(south, xs)])
    from_south = [s * x for s, x in zip(south, south_list(xs))]
    out = []
    for j, x in enumerate(xs):
        out.append((west_of(east[j] * x) + east[j] * east_of(x)) + (from_north[j] + from_south[j]))
    return out


GROUPS = 9
PLANES = 6
MIB = 1024 * 1024
START, STORAGE, LEAKAGE, EAST, SOUTH, WEIGHT = range(PLANES)


def tile_of(k):
    return slice(k * LANES, (k + 1) * LANES)


def rows_of(g):
    return slice(g * SUB, (g + 1) * SUB)


def rows(j):
    return pl.ds(j, SUB, stride=STRIDE)


def rolled(x, amount):
    return pltpu.roll(x, lax.rem(amount + 4 * LANES, LANES), 1)


def half_turn(x):
    return pltpu.roll(x, SUB // 2, 0)


def whole(shape):
    return pl.BlockSpec(shape, lambda i: (0,) * len(shape))


def edge_rows_kernel(
    flags, prev, source, start, storage, leakage, east, south, weight, coef, to_up, to_down, waves, planes, numbers, sems
):
    total = prev.shape[0]
    lanes, sub = lane_ids(), sub_ids()
    copies = []

    def fetch(source_ref, target_ref):
        copies.append(pltpu.make_async_copy(source_ref, target_ref, sems.at[len(copies)]))
        copies[-1].start()

    for end, g in ((0, 0), (1, SUB - 1)):
        for array, ref in ((0, prev), (1, source)):
            fetch(ref.at[:, rows_of(g), :], waves.at[array, end])
    for p, ref in enumerate((start, storage, leakage, east, south)):
        fetch(ref, planes.at[p])
    fetch(weight, numbers)
    for copy in copies:
        copy.wait()

    def slabs(slab, even, odd):
        for k in range(2):
            to_up[slab, :, tile_of(k)] = jnp.where(sub < 4, even(0, k), half_turn(odd(0, k)))
            to_down[slab, :, tile_of(k)] = jnp.where(sub < 4, half_turn(odd(1, k)), even(1, k))

    for p in range(PLANES):
        for g in range(SUB):
            for k in range(2):
                ref = numbers if p == WEIGHT else planes.at[p]
                value = ref[rows_of(g), tile_of(k)].astype(jnp.float32)
                if p == EAST and k == 1:
                    value = jnp.where((lanes == LANES - 1) & (flags[1] == 0), 0.0, value)
                if p == SOUTH and g == SUB - 1:
                    value = jnp.where((sub == SUB - 1) & (flags[3] == 0), 0.0, value)
                coef[p, rows_of(g), tile_of(k)] = value

    plane = lambda p: lambda end, k: coef[p, rows_of(end * (SUB - 1)), tile_of(k)]
    for q in range(PLANES // 2):
        slabs(total + q, plane(2 * q), plane(2 * q + 1))

    def pair(q, _):
        for array in range(2):
            wave = lambda i: lambda end, k: waves[array, end, i, :, tile_of(k)]
            slabs(array * (total // 2) + q, wave(2 * q), wave(2 * q + 1))
        return 0

    lax.fori_loop(0, total // 2, pair, 0)


def edge_rows(flags, prev, source, planes):
    steps, nr, nc = prev.shape
    out = jax.ShapeDtypeStruct((steps + PLANES // 2, SUB, nc), jnp.float32)
    vmem = pl.BlockSpec(memory_space=pltpu.VMEM)
    return pl.pallas_call(
        edge_rows_kernel,
        in_specs=[pl.BlockSpec(memory_space=pltpu.SMEM)] + [pl.BlockSpec(memory_space=pltpu.HBM)] * (2 + PLANES),
        out_specs=[vmem, vmem, vmem],
        out_shape=[jax.ShapeDtypeStruct((PLANES, nr, nc), jnp.float32), out, out],
        scratch_shapes=[
            pltpu.VMEM((2, 2, steps, SUB, nc), jnp.float32),
            pltpu.VMEM((PLANES - 1, nr, nc), jnp.float32),
            pltpu.VMEM((nr, nc), jnp.int32),
            pltpu.SemaphoreType.DMA((PLANES + 4,)),
        ],
        compiler_params=pltpu.CompilerParams(vmem_limit_bytes=60 * MIB),
        name="rows",
    )(flags, prev, source, *planes)


def put_sides(left, right, array, slot, g, value_left, value_right):
    lanes = lane_ids()
    here = (lanes >= slot) & (lanes < slot + 3)
    left[array, rows_of(g), :] = jnp.where(here, rolled(value_left, slot), left[array, rows_of(g), :])
    right[array, rows_of(g), :] = jnp.where(here, rolled(value_right, slot + 3), right[array, rows_of(g), :])


def pack_kernel(prev, source, coef, to_left, to_right):
    step0 = pl.program_id(0)
    steps = prev.shape[0]

    @pl.when(step0 == 0)
    def _():
        for array in range(3):
            to_left[array] = jnp.zeros_like(to_left[array])
            to_right[array] = jnp.zeros_like(to_right[array])
        for p in range(PLANES):
            for g in range(SUB):
                put_sides(to_left, to_right, 2, 4 * p, g, *[coef[p, rows_of(g), tile_of(k)] for k in range(2)])

    def step(i, _):
        for array, ref in ((0, prev), (1, source)):
            for g in range(SUB):
                values = [ref[i, rows_of(g), tile_of(k)] for k in range(2)]
                put_sides(to_left, to_right, array, 4 * (step0 * steps + i), g, *values)
        return 0

    lax.fori_loop(0, steps, step, 0)


def pack(prev, source, coefs):
    steps, nr, nc = prev.shape
    block = 8
    big = pl.BlockSpec((block, nr, nc), lambda i: (i, 0, 0))
    shape = (3, nr, LANES)
    return pl.pallas_call(
        pack_kernel,
        grid=(steps // block,),
        in_specs=[big, big, whole(coefs.shape)],
        out_specs=[whole(shape)] * 2,
        out_shape=[jax.ShapeDtypeStruct(shape, jnp.float32)] * 2,
        compiler_params=pltpu.CompilerParams(vmem_limit_bytes=16 * MIB),
        cost_estimate=pl.CostEstimate(flops=20_000_000, bytes_accessed=16_000_000, transcendentals=0),
        name="pack",
    )(prev, source, coefs)


def corners_kernel(flags, left, right, yA, yB, to_left, to_right):
    total = yA.shape[0] - PLANES // 2
    sub = sub_ids()
    for array in range(3):
        for ref, out in ((left, to_left), (right, to_right)):
            out[array, : SUB * SUB, :] = ref[array]
            out[array, rows_of(SUB), :] = jnp.zeros((SUB, LANES), jnp.float32)

    def both(slab, array, slot):
        for odd in range(2):
            values = [halo_rows(yB[slab, :, tile_of(k)], yA[slab, :, tile_of(k)], odd, sub) for k in range(2)]
            put_sides(to_left, to_right, array, slot + 4 * odd, SUB, *values)

    for q in range(PLANES // 2):
        for odd in range(2):
            values = [
                halo_rows(
                    present(yB[total + q, :, tile_of(k)], flags[3]), present(yA[total + q, :, tile_of(k)], flags[2]), odd, sub
                )
                for k in range(2)
            ]
            put_sides(to_left, to_right, 2, 4 * (2 * q + odd), SUB, *values)

    def pair(q, _):
        for array in range(2):
            both(array * (total // 2) + q, array, 8 * q)
        return 0

    lax.fori_loop(0, total // 2, pair, 0)


def corners(flags, left, right, yA, yB):
    vmem = pl.BlockSpec(memory_space=pltpu.VMEM)
    out = jax.ShapeDtypeStruct((3, GROUPS * SUB, LANES), jnp.float32)
    return pl.pallas_call(
        corners_kernel,
        in_specs=[pl.BlockSpec(memory_space=pltpu.SMEM)] + [vmem] * 4,
        out_specs=[vmem, vmem],
        out_shape=[out, out],
        compiler_params=pltpu.CompilerParams(vmem_limit_bytes=8 * MIB),
        name="corners",
    )(flags, left, right, yA, yB)


def windows_of(left, right, halo_left, halo_right, lanes):
    return (
        jnp.where(lanes < LANES - 3, left, halo_left),
        jnp.where(lanes < LANES // 2, right, left),
        jnp.where(lanes < 3, halo_right, right),
    )


def halo_rows(below, above, odd, sub):
    if odd:
        return half_turn(jnp.where(sub < 4, above, below))
    return jnp.where(sub < 4, below, above)


def present(x, flag):
    return jnp.where(flag != 0, x, 0.0)


def sweep_kernel(flags, prev, source, coefs, xL, xR, yA, yB, out, rims, yU, yD, tiles, ctiles, halo, coef, carry):
    step0 = pl.program_id(0)
    steps = prev.shape[0]
    total = steps * pl.num_programs(0)
    lanes, sub = lane_ids(), sub_ids()

    def window_set(j, left, right, array, slot):
        return windows_of(
            left, right, rolled(halo[0, array, rows(j), :], LANES - 3 - slot), rolled(halo[1, array, rows(j), :], -slot), lanes
        )

    breaks = (LANES - 4, LANES // 2 - 1, 2)
    outer = (LANES - 3, -1, 2)

    @pl.when(step0 == 0)
    def _():
        for array in range(3):
            for side, ref in ((0, xL), (1, xR)):
                for g in range(GROUPS):
                    value = ref[array, rows_of(g), :]
                    halo[side, array, rows_of(g), :] = present(value, flags[side]) if array == 2 else value
        for p in range(5):
            slab = total + p // 2
            for k in range(2):
                for g in range(SUB):
                    ctiles[p, k, rows_of(g), :] = coefs[p, rows_of(g), tile_of(k)]
                ctiles[p, k, rows_of(SUB), :] = halo_rows(
                    present(yB[slab, :, tile_of(k)], flags[3]), present(yA[slab, :, tile_of(k)], flags[2]), p % 2, sub
                )
        planes = [
            [window_set(j, ctiles[p, 0, rows(j), :], ctiles[p, 1, rows(j), :], 2, 4 * p) for j in range(STRIDE)]
            for p in range(5)
        ]
        for w in range(3):
            start, storage, leakage, east, south = [[planes[p][j][w] for j in range(STRIDE)] for p in range(5)]
            east = [jnp.where(lanes == breaks[w], 0.0, e) for e in east]
            north = north_list(south)
            diag, scale = [], []
            for j in range(STRIDE):
                d = storage[j] + leakage[j] + east[j] + west_of(east[j]) + south[j] + north[j]
                row = row_ids_of(j)
                inner = ((row < 66) | (row > 69)) & (lanes != outer[w]) & (d > 0.0)
                diag.append(d)
                scale.append(jnp.where(inner, 1.0 / jnp.sqrt(jnp.where(inner, d, 1.0)), 0.0))
            scale_south = south_list(scale)
            for j in range(STRIDE):
                carry[w, j] = start[j]
                coef[0, w, j] = east[j] * scale[j] * east_of(scale[j])
                coef[1, w, j] = south[j] * scale[j] * scale_south[j]
                coef[2, w, j] = storage[j]
                coef[3, w, j] = diag[j]
                coef[4, w, j] = east[j]
                coef[5, w, j] = south[j]
                coef[6, w, j] = scale[j]
                coef[7, w, j] = scale[j] * np.float32(Q_COEF[3])
        for side in range(2):
            rims[side] = jnp.zeros_like(rims[side])

    def step(i, t, odd):
        for array, ref in ((0, prev), (1, source)):
            slab = array * (total // 2) + t // 2
            for k in range(2):
                for g in range(SUB):
                    tiles[odd, array, k, rows_of(g), :] = ref[i, rows_of(g), tile_of(k)]
                tiles[odd, array, k, rows_of(SUB), :] = halo_rows(yB[slab, :, tile_of(k)], yA[slab, :, tile_of(k)], odd, sub)
        x0s, srcs = [
            [window_set(j, tiles[odd, a, 0, rows(j), :], tiles[odd, a, 1, rows(j), :], a, 4 * t) for j in range(STRIDE)]
            for a in range(2)
        ]
        every = range(3)
        x0 = [[x0s[j][w] for j in range(STRIDE)] for w in every]
        table = lambda n, w: [coef[n, w, j] for j in range(STRIDE)]
        full = [off_diagonal(x0[w], table(4, w), table(5, w)) for w in every]
        z = [
            [
                coef[6, w, j] * ((srcs[j][w] + coef[2, w, j] * carry[w, j]) + (full[w][j] - coef[3, w, j] * x0[w][j]))
                for j in range(STRIDE)
            ]
            for w in every
        ]
        apply = lambda v: [off_diagonal(v[w], table(0, w), table(1, w)) for w in every]
        base = [[a + b for a, b in zip(p, q)] for p, q in zip(z, apply(z))]
        y = base
        for k in (2, 1, 0):
            y = apply(apply(y))
            ratio = np.float32(Q_COEF[k] / Q_COEF[3])
            y = [[a + ratio * b for a, b in zip(p, q)] for p, q in zip(y, base)]
        result = [[x0[w][j] + coef[7, w, j] * y[w][j] for j in range(STRIDE)] for w in every]
        slot = 4 * t
        here = (lanes >= slot) & (lanes < slot + 3)
        for j in range(STRIDE):
            a, b, c = result[0][j], result[1][j], result[2][j]
            left = jnp.where(lanes < 96, a, b)
            right = jnp.where(lanes < 32, b, c)
            out[i, 0, rows(j), :] = left
            out[i, 1, rows(j), :] = right
            fresh = windows_of(left, right, a, c, lanes)
            for w in range(3):
                carry[w, j] = fresh[w]
            rims[0, rows(j), :] = jnp.where(here, rolled(a, slot + 2), rims[0, rows(j), :])
            rims[1, rows(j), :] = jnp.where(here, rolled(c, slot + 1), rims[1, rows(j), :])

    def pair(q, _):
        for odd in range(2):
            step(2 * q + odd, step0 * steps + 2 * q + odd, odd)
        kept = (sub < 2) | (sub > 5)
        slab = step0 * (steps // 2) + q
        for k in range(2):
            down, up = [], []
            for odd in range(2):
                first, last, beyond = [out[2 * q + odd, k, rows_of(g), :] for g in (0, SUB - 1, SUB)]
                down.append(jnp.where(sub < 4, beyond, last))
                up.append(jnp.where(sub < 4, first, beyond))
            yD[slab, :, tile_of(k)] = jnp.where(kept, down[0], half_turn(down[1]))
            yU[slab, :, tile_of(k)] = jnp.where(kept, up[0], half_turn(up[1]))
        return 0

    lax.fori_loop(0, steps // 2, pair, 0)

    @pl.when(step0 == pl.num_programs(0) - 1)
    def _():
        for side in range(2):
            first, last, beyond = [rims[side, rows_of(g), :] for g in (0, SUB - 1, SUB)]
            yD[total // 2, :, tile_of(side)] = jnp.where(sub < 4, beyond, last)
            yU[total // 2, :, tile_of(side)] = jnp.where(sub < 4, first, beyond)


def sweep(flags, prev, source, coefs, xL, xR, yA, yB):
    steps, nr, nc = prev.shape
    block = 4
    big = pl.BlockSpec((block, nr, nc), lambda i: (i, 0, 0))
    ext = GROUPS * SUB
    consts = (coefs, xL, xR, yA, yB)
    rest = [(2, ext, LANES), (steps // 2 + 2, SUB, nc), (steps // 2 + 2, SUB, nc)]
    return pl.pallas_call(
        sweep_kernel,
        grid=(steps // block,),
        in_specs=[pl.BlockSpec(memory_space=pltpu.SMEM), big, big] + [whole(a.shape) for a in consts],
        out_specs=[pl.BlockSpec((block, 2, ext, LANES), lambda i: (i, 0, 0, 0))] + [whole(s) for s in rest],
        out_shape=[jax.ShapeDtypeStruct(s, jnp.float32) for s in [(steps, 2, ext, LANES)] + rest],
        scratch_shapes=[
            pltpu.VMEM((2, 2, 2, ext, LANES), jnp.float32),
            pltpu.VMEM((5, 2, ext, LANES), jnp.float32),
            pltpu.VMEM((2, 3, ext, LANES), jnp.float32),
            pltpu.VMEM((8, 3, STRIDE, SUB, LANES), jnp.float32),
            pltpu.VMEM((3, STRIDE, SUB, LANES), jnp.float32),
        ],
        compiler_params=pltpu.CompilerParams(vmem_limit_bytes=16 * MIB),
        name="sweep",
    )(flags, prev, source, *consts)


def split3(x):
    hi = x.astype(jnp.bfloat16)
    left = x - hi.astype(jnp.float32)
    mid = left.astype(jnp.bfloat16)
    low = (left - mid.astype(jnp.float32)).astype(jnp.bfloat16)
    return hi, mid, low


def settle_kernel(
    flags, local, source, coefs, xL, xR, yA, yB, rims, rL, rR, kA, kB, ids, settled, coarse, pack, ring, edge, before, resid
):
    step0 = pl.program_id(0)
    steps = local.shape[0]
    total = steps * pl.num_programs(0)
    lanes, sub = lane_ids(), sub_ids()
    has_left, has_right, has_up, has_down = [(flags[k] != 0) for k in range(4)]
    as_one = lambda mask: jnp.where(mask, 1.0, 0.0)
    only = lambda mask, x: jnp.where(mask, x, 0.0)

    def column(ref, g, lane):
        return jnp.broadcast_to(ref[2, rows_of(g), lane : lane + 1], (SUB, LANES))

    def halo_plane(p, k):
        slab = total + p // 2
        return halo_rows(
            present(yB[slab, :, tile_of(k)], flags[3]), present(yA[slab, :, tile_of(k)], flags[2]), p % 2, sub
        )

    @pl.when(step0 == 0)
    def _():
        across = lambda k: as_one((lanes < 2) & has_left) if k == 0 else as_one((lanes > LANES - 3) & has_right)
        for g in range(GROUPS):
            if g < SUB:
                down = only(sub < 2, as_one(has_up)) if g == 0 else only(sub > 5, as_one(has_down)) if g == SUB - 1 else 0.0 * as_one(sub < 0)
            else:
                down = as_one(sub >= 0)
            for k in range(2):
                copies = (1.0 + across(k)) * (1.0 + down) - 1.0
                weight = coefs[WEIGHT, rows_of(g), tile_of(k)] if g < SUB else halo_plane(WEIGHT, k)
                ring[0, k, g] = weight / (weight + copies)
                ring[1, k, g] = 1.0 / (weight + copies)
            for side, got, xref, lane, keep, back in ((0, rL, xL, 4 * WEIGHT + 2, 0, LANES - 1), (1, rR, xR, 4 * WEIGHT, 2, 1)):
                arrived = present(got[rows_of(g), :], flags[side])
                fwd_above = present(kA[total // 2 + 1, :, tile_of(side)], flags[side] * flags[2])
                fwd_below = present(kB[total // 2 + 1, :, tile_of(side)], flags[side] * flags[3])
                if g == 0:
                    extra = only(sub < 2, fwd_above)
                elif g == SUB - 1:
                    extra = only(sub > 5, fwd_below)
                elif g == SUB:
                    extra = only(sub == SUB - 1, fwd_above) + only(sub == 0, fwd_below)
                else:
                    extra = jnp.zeros((SUB, LANES), jnp.float32)
                value = arrived + extra
                if g < SUB:
                    mine = rims[side, rows_of(g), :]
                    if g == 0:
                        mine = mine + only((sub < 2) & has_up, kA[total // 2, :, tile_of(side)])
                    if g == SUB - 1:
                        mine = mine + only((sub > 5) & has_down, kB[total // 2, :, tile_of(side)])
                    weight = column(xref, g, lane)
                    copies = 2.0 * (1.0 + down) - 1.0
                    outer = (weight * arrived + (pltpu.roll(mine, back, 1) + extra)) / (weight + copies)
                    value = jnp.where(lax.rem(lanes, 4) == keep, outer, value)
                edge[side, g] = value
        for k in range(2):
            for g in range(SUB):
                own = lambda p: coefs[p, rows_of(g), tile_of(k)]
                neighbour = present(column(xL, g, 4 * EAST + 2), flags[0]) if k == 0 else coefs[EAST, rows_of(g), tile_of(0)]
                west = west_of(jnp.where(lanes == LANES - 1, neighbour, own(EAST)))
                above = halo_plane(SOUTH, k) if g == 0 else coefs[SOUTH, rows_of(g - 1), tile_of(k)]
                north = pltpu.roll(jnp.where(sub == SUB - 1, above, own(SOUTH)), 1, 0)
                pack[0, k, g] = west
                pack[1, k, g] = north
                pack[2, k, g] = own(STORAGE) + own(LEAKAGE) + own(EAST) + west + own(SOUTH) + north
                before[k, g] = own(START)

    def step(i, t, odd):
        slab = t // 2
        mid = []
        for k in range(2):
            from_above, from_below = kA[slab, :, tile_of(k)], kB[slab, :, tile_of(k)]
            if odd:
                from_above, from_below = half_turn(from_above), half_turn(from_below)
            values = []
            for g in range(GROUPS):
                side = rolled(edge[k, g], -4 * t - 1 if k == 0 else LANES - 2 - 4 * t)
                extra = only(lanes < 2 if k == 0 else lanes > LANES - 3, side)
                here = local[i, k, rows_of(g), :]
                if g == 0:
                    extra = extra + only((sub < 2) & has_up, from_above)
                elif g == SUB - 1:
                    extra = extra + only((sub > 5) & has_down, from_below)
                elif g == SUB:
                    extra = extra + here
                    here = jnp.where(sub < 4, from_below, from_above)
                values.append((ring[0, k, g] * here + ring[1, k, g] * extra, side))
            mid.append(values)
        for k in range(2):
            for g in range(SUB):
                x = mid[k][g][0]
                if k == 0:
                    west = jnp.where(lanes == LANES - 1, mid[0][g][1], x)
                    east = jnp.where(lanes == 0, mid[1][g][0], x)
                else:
                    west = jnp.where(lanes == LANES - 1, mid[0][g][0], x)
                    east = jnp.where(lanes == 0, mid[1][g][1], x)
                north = jnp.where(sub == SUB - 1, mid[k][(g + GROUPS - 1) % GROUPS][0], x)
                south = jnp.where(sub == 0, mid[k][g + 1][0], x)
                around = (coefs[EAST, rows_of(g), tile_of(k)] * east_of(east) + pack[0, k, g] * west_of(west)) + (
                    coefs[SOUTH, rows_of(g), tile_of(k)] * pltpu.roll(south, SUB - 1, 0) + pack[1, k, g] * pltpu.roll(north, 1, 0)
                )
                value = (source[i, rows_of(g), tile_of(k)] + coefs[STORAGE, rows_of(g), tile_of(k)] * before[k, g]) - (
                    pack[2, k, g] * x - around
                )
                resid[k, pl.ds(t * 64 + g * SUB, SUB), :] = value
                before[k, g] = x
                settled[i, rows_of(g), tile_of(k)] = x

    def pair(q, _):
        for odd in range(2):
            step(2 * q + odd, step0 * steps + 2 * q + odd, odd)
        return 0

    lax.fori_loop(0, steps // 2, pair, 0)

    @pl.when(step0 == pl.num_programs(0) - 1)
    def _():
        aggs = lax.broadcasted_iota(jnp.int32, (64, 2 * LANES), 0)

        def one_row(r, acc):
            picked = jnp.broadcast_to(ids[pl.ds(r, 1), :] - flags[4], (64, 2 * LANES))
            hot = jnp.where(picked == aggs, 1.0, 0.0).astype(jnp.bfloat16)
            values = jnp.concatenate([resid[k, pl.ds(r, total, stride=64), :] for k in range(2)], axis=1)
            parts = jnp.concatenate(split3(values), axis=0)
            return acc + lax.dot_general(parts, hot, (((1,), (1,)), ((), ())), preferred_element_type=jnp.float32)

        def rows4(r, acc):
            for o in range(4):
                acc = one_row(4 * r + o, acc)
            return acc

        acc = lax.fori_loop(0, 16, rows4, jnp.zeros((3 * total, 64), jnp.float32))
        sums = acc[:total] + acc[total : 2 * total] + acc[2 * total :]
        block = jnp.concatenate([sums[: total // 2], sums[total // 2 :]], axis=1)
        coarse[0] = block


def settle(flags, local, source, coefs, xL, xR, yA, yB, rims, rL, rR, kA, kB, ids):
    steps, nr, nc = source.shape
    block = 4
    ext = GROUPS * SUB
    big = pl.BlockSpec((block, nr, nc), lambda i: (i, 0, 0))
    consts = (coefs, xL, xR, yA, yB, rims, rL, rR, kA, kB, ids)
    shapes = [(steps, nr, nc), (1, steps // 2, LANES)]
    return pl.pallas_call(
        settle_kernel,
        grid=(steps // block,),
        in_specs=[
            pl.BlockSpec(memory_space=pltpu.SMEM),
            pl.BlockSpec((block, 2, ext, LANES), lambda i: (i, 0, 0, 0)),
            big,
        ]
        + [whole(a.shape) for a in consts],
        out_specs=[big, whole(shapes[1])],
        out_shape=[jax.ShapeDtypeStruct(s, jnp.float32) for s in shapes],
        scratch_shapes=[
            pltpu.VMEM((3, 2, SUB, SUB, LANES), jnp.float32),
            pltpu.VMEM((2, 2, GROUPS, SUB, LANES), jnp.float32),
            pltpu.VMEM((2, GROUPS, SUB, LANES), jnp.float32),
            pltpu.VMEM((2, SUB, SUB, LANES), jnp.float32),
            pltpu.VMEM((2, steps * nr, LANES), jnp.float32),
        ],
        compiler_params=pltpu.CompilerParams(vmem_limit_bytes=20 * MIB),
        name="settle",
    )(flags, local, source, *consts)


def finish_kernel(flags, every, inverse, settled, ids, out, table, stacked):
    step0 = pl.program_id(0)
    steps = settled.shape[0]
    half = every.shape[1]
    lanes = lane_ids()

    @pl.when(step0 == 0)
    def _():
        for d in range(every.shape[0] // 2):
            for g in range(half // SUB):
                a, b = [every[2 * d + o, rows_of(g), :] for o in range(2)]
                stacked[rows_of(g), tile_of(d)] = jnp.where(lanes < LANES // 2, a, pltpu.roll(b, LANES // 2, 1))
                stacked[half + g * SUB : half + (g + 1) * SUB, tile_of(d)] = jnp.where(
                    lanes < LANES // 2, pltpu.roll(a, LANES // 2, 1), b
                )
        product = lax.dot_general(
            stacked[...],
            inverse[...],
            (((1,), (1,)), ((), ())),
            precision=lax.Precision.HIGHEST,
            preferred_element_type=jnp.float32,
        )
        table[...] = jnp.concatenate([product, product], axis=1)

    def step(i, _):
        t = step0 * steps + i
        row = jnp.broadcast_to(table[pl.ds(t, 1), :], (SUB, LANES))
        for g in range(SUB):
            for k in range(2):
                picked = ids[rows_of(g), tile_of(k)] - flags[4]
                out[i, rows_of(g), tile_of(k)] = settled[i, rows_of(g), tile_of(k)] + jnp.take_along_axis(row, picked, axis=1)
        return 0

    lax.fori_loop(0, steps, step, 0, unroll=True)


def finish(flags, every, inverse, settled, ids):
    steps, nr, nc = settled.shape
    block = 8
    big = pl.BlockSpec((block, nr, nc), lambda i: (i, 0, 0))
    return pl.pallas_call(
        finish_kernel,
        grid=(steps // block,),
        in_specs=[pl.BlockSpec(memory_space=pltpu.SMEM), whole(every.shape), whole(inverse.shape), big, whole(ids.shape)],
        out_specs=big,
        out_shape=jax.ShapeDtypeStruct(settled.shape, jnp.float32),
        scratch_shapes=[pltpu.VMEM((steps, LANES), jnp.float32), pltpu.VMEM((steps, inverse.shape[1]), jnp.float32)],
        compiler_params=pltpu.CompilerParams(vmem_limit_bytes=20 * MIB),
        name="finish",
    )(flags, every, inverse, settled, ids)


def neighbours(low, high, axis):
    count = lax.axis_size(axis)
    forward = [(i, (i + 1) % count) for i in range(count)]
    backward = [(target, source) for source, target in forward]
    return lax.ppermute(high, axis, forward), lax.ppermute(low, axis, backward)


def gather_all(block):
    count = lax.axis_size("gx") * lax.axis_size("gy")
    block = block.reshape(1, 1, -1)
    every = lax.all_to_all(jnp.broadcast_to(block, (count,) + block.shape[1:]), ("gx", "gy"), 0, 0)
    return every.reshape(count, -1, LANES)


def shards(
    prev_wave,
    source,
    start_state,
    storage,
    leakage,
    cond_east,
    cond_south,
    owner_weight,
    aggregate,
    coarse_inverse,
):
    gx, gy = lax.axis_index("gx"), lax.axis_index("gy")
    nx, ny = lax.axis_size("gx"), lax.axis_size("gy")
    flags = jnp.stack([gx, nx - 1 - gx, gy, ny - 1 - gy, (gx * ny + gy) * coarse_inverse.shape[0]]).astype(jnp.int32)
    planes = (start_state, storage, leakage, cond_east, cond_south, owner_weight)
    coefs, to_up, to_down = edge_rows(flags, prev_wave, source, planes)
    yA, yB = neighbours(to_up, to_down, "gy")
    to_left, to_right = pack(prev_wave, source, coefs)
    to_left, to_right = corners(flags, to_left, to_right, yA, yB)
    xL, xR = neighbours(to_left, to_right, "gx")
    local, rims, yU, yD = sweep(flags, prev_wave, source, coefs, xL, xR, yA, yB)
    rL, rR = neighbours(rims[0], rims[1], "gx")
    half = SUB // 2
    around = jnp.concatenate([rL, rR], -1)
    yU = yU.at[-1].set(jnp.concatenate([around[:half], around[-half:]], 0))
    yD = yD.at[-1].set(jnp.concatenate([around[-SUB : -half], around[-SUB - half : -SUB]], 0))
    kA, kB = neighbours(yU, yD, "gy")
    settled, coarse = settle(flags, local, source, coefs, xL, xR, yA, yB, rims, rL, rR, kA, kB, aggregate)
    every = gather_all(coarse)
    return finish(flags, every, coarse_inverse, settled, aggregate)


def solution(mesh):
    return jax.shard_map(
        shards,
        mesh=mesh,
        in_specs=(
            P(None, "gy", "gx"),
            P(None, "gy", "gx"),
            P("gy", "gx"),
            P("gy", "gx"),
            P("gy", "gx"),
            P("gy", "gx"),
            P("gy", "gx"),
            P("gy", "gx"),
            P("gy", "gx"),
            P(("gx", "gy"), None),
        ),
        out_specs=P(None, "gy", "gx"),
        check_vma=False,
    )
```
